32 devices in a mesh: dp: 8 (over z, x), mp: 4 (over y, core).
Axes of the slice: x: 2, y: 2, z: 4, core: 2. Of those that a mesh axis runs over, the one named last changes fastest.
Arguments:
- tokens: bfloat16 [16384, 1024], P(('dp', 'mp')), may hold values from -6 to 6
- cotangent: bfloat16 [16384, 1024], P(('dp', 'mp'))
- lengths: int32 [8, 4], P('dp'), may hold values from 0 to 2048, as said below
- attend: float32 [3, 1024, 1024], P(None, 'dp', 'mp'), may hold values from -0.1875 to 0.1875
- mixing: float32 [1024, 1024], P('mp', 'dp'), may hold values from -0.1875 to 0.1875
- expand: float32 [1024, 4096], P('dp', 'mp'), may hold values from -0.1875 to 0.1875
- contract: float32 [4096, 1024], P('mp', 'dp'), may hold values from -0.09375 to 0.09375
- outer_norms: float32 [4, 1024], P(None, ('dp', 'mp'))
- head_norms: float32 [2, 1024], P(None, ('dp', 'mp'))
- unit_norms: float32 [2, 4096], P(None, ('dp', 'mp'))
- attend_moment: float32 [3, 1024, 1024], P(None, 'dp', 'mp'), may hold values from -0.00018310547 to 0.00018310547
- mixing_moment: float32 [1024, 1024], P('mp', 'dp'), may hold values from -0.00018310547 to 0.00018310547
- expand_moment: float32 [1024, 4096], P('dp', 'mp'), may hold values from -0.00018310547 to 0.00018310547
- contract_moment: float32 [4096, 1024], P('mp', 'dp'), may hold values from -0.00018310547 to 0.00018310547
- outer_moment: float32 [4, 1024], P(None, ('dp', 'mp')), may hold values from -0.00018310547 to 0.00018310547
- head_moment: float32 [2, 1024], P(None, ('dp', 'mp')), may hold values from -0.00018310547 to 0.00018310547
- unit_moment: float32 [2, 4096], P(None, ('dp', 'mp')), may hold values from -0.00018310547 to 0.00018310547
- attend_square: float32 [3, 1024, 1024], P(None, 'dp', 'mp'), may hold values from 1e-09 to 1.6e-08
- mixing_square: float32 [1024, 1024], P('mp', 'dp'), may hold values from 1e-09 to 1.6e-08
- expand_square: float32 [1024, 4096], P('dp', 'mp'), may hold values from 1e-09 to 1.6e-08
- contract_square: float32 [4096, 1024], P('mp', 'dp'), may hold values from 1e-09 to 1.6e-08
- outer_square: float32 [4, 1024], P(None, ('dp', 'mp')), may hold values from 1e-09 to 1.6e-08
- head_square: float32 [2, 1024], P(None, ('dp', 'mp')), may hold values from 1e-09 to 1.6e-08
- unit_square: float32 [2, 4096], P(None, ('dp', 'mp')), may hold values from 1e-09 to 1.6e-08
Outputs:
- output: bfloat16 [16384, 1024], P(('dp', 'mp'))
- input_grad: float32 [16384, 1024], P(('dp', 'mp'))
- grad_norm: float32 [], replicated
- attend_grad: float32 [3, 1024, 1024], P(None, 'dp', 'mp')
- attend_moment_new: float32 [3, 1024, 1024], P(None, 'dp', 'mp')
- attend_square_new: float32 [3, 1024, 1024], P(None, 'dp', 'mp')
- attend_change: float32 [3, 1024, 1024], P(None, 'dp', 'mp')
- mixing_grad: float32 [1024, 1024], P('mp', 'dp')
- mixing_moment_new: float32 [1024, 1024], P('mp', 'dp')
- mixing_square_new: float32 [1024, 1024], P('mp', 'dp')
- mixing_change: float32 [1024, 1024], P('mp', 'dp')
- expand_grad: float32 [1024, 4096], P('dp', 'mp')
- expand_moment_new: float32 [1024, 4096], P('dp', 'mp')
- expand_square_new: float32 [1024, 4096], P('dp', 'mp')
- expand_change: float32 [1024, 4096], P('dp', 'mp')
- contract_grad: float32 [4096, 1024], P('mp', 'dp')
- contract_moment_new: float32 [4096, 1024], P('mp', 'dp')
- contract_square_new: float32 [4096, 1024], P('mp', 'dp')
- contract_change: float32 [4096, 1024], P('mp', 'dp')
- outer_grad: float32 [4, 1024], P(None, ('dp', 'mp'))
- outer_moment_new: float32 [4, 1024], P(None, ('dp', 'mp'))
- outer_square_new: float32 [4, 1024], P(None, ('dp', 'mp'))
- outer_change: float32 [4, 1024], P(None, ('dp', 'mp'))
- head_grad: float32 [2, 1024], P(None, ('dp', 'mp'))
- head_moment_new: float32 [2, 1024], P(None, ('dp', 'mp'))
- head_square_new: float32 [2, 1024], P(None, ('dp', 'mp'))
- head_change: float32 [2, 1024], P(None, ('dp', 'mp'))
- unit_grad: float32 [2, 4096], P(None, ('dp', 'mp'))
- unit_moment_new: float32 [2, 4096], P(None, ('dp', 'mp'))
- unit_square_new: float32 [2, 4096], P(None, ('dp', 'mp'))
- unit_change: float32 [2, 4096], P(None, ('dp', 'mp'))
The draws below stay inside these ranges and needn't reach their ends.
Inputs may be any that keep to these rules, and one draw needn't show every extreme that they name: Row g lists the lengths of up to 4 sequences packed in order from the first slot of group g; a row sums to at most 2048, and the slots after its sum are padding. In every draw one sequence fills all 2048 slots of some group.
All inputs are finite; a program needn't handle non-finite values.
Results may differ from the reference program's by a relative error of at most 0.0181.
Values may be sent and summed in bfloat16 or wider, within the bound.
No kernel may reach another device: no remote copies, remote signals or barrier semaphores. Data moves between devices by JAX's collectives and lax.ppermute only.
A program may use at most 192 MiB of HBM per device.

```python
import math
import jax
import jax.numpy as jnp
from jax import lax

D = 1024
HEADS = 16
HD = 64
FF = 4096
TOK_DEV = 2048
SEQS = 4
MINLEN = 64
ADAM_STEP = 10
GROUPS = 8
TOKENS = 16384


def column_ramp(width):
    places = jnp.arange(width, dtype=jnp.float32) / (width - 1)
    return 0.5 + places


def norm_table(key, height, width, ramped):
    gain_key, bias_key = jax.random.split(key)
    gains = 1.0 + 0.4 * jax.random.uniform(gain_key, (height // 2, width), jnp.float32, -1.0, 1.0)
    biases = 0.3 * jax.random.normal(bias_key, (height // 2, width), jnp.float32)
    if ramped:
        gains = gains * column_ramp(width)[None, :]
    return jnp.stack([gains, biases], axis=1).reshape(height, width)


def draw_cotangent(key, part):
    noise_key = jax.random.fold_in(key, 15)
    values = jnp.clip(jax.random.normal(noise_key, (TOKENS, D), jnp.float32), -6.0, 6.0)
    return (values * column_ramp(D)[None, :]).astype(jnp.bfloat16)


def draw_outer_norms(key, part):
    return norm_table(jax.random.fold_in(key, 11), 4, D, True)


def draw_head_norms(key, part):
    return norm_table(jax.random.fold_in(key, 12), 2, D, False)


def draw_unit_norms(key, part):
    return norm_table(jax.random.fold_in(key, 13), 2, FF, False)


def draw_lengths(key, part):
    power_key, extra_key, pick_key = jax.random.split(jax.random.fold_in(key, 14), 3)
    powers = jax.random.randint(power_key, (GROUPS, SEQS), 0, 5)
    base = MINLEN * jnp.left_shift(jnp.ones((GROUPS, SEQS), jnp.int32), powers)
    wanted = base + jax.random.randint(extra_key, (GROUPS, SEQS), 0, base)
    chosen = jax.random.randint(pick_key, (), 0, GROUPS)
    first = (jnp.arange(GROUPS)[:, None] == chosen) & (jnp.arange(SEQS)[None, :] == 0)
    wanted = jnp.where(first, TOK_DEV, wanted).astype(jnp.int32)
    starts = jnp.cumsum(wanted, axis=1) - wanted
    return jnp.minimum(jnp.maximum(TOK_DEV - starts, 0), wanted).astype(jnp.int32)


def shard_levels(key, extent, pieces, smallest, high):
    level, own = 1.0, jax.random.fold_in(key, 6)
    for axis_at, blocks in pieces:
        heights = jnp.exp(jax.random.uniform(jax.random.fold_in(own, axis_at), (blocks,), jnp.float32, smallest / len(pieces), high / len(pieces)))
        level = level * jnp.repeat(heights, extent[axis_at] // blocks).reshape([-1 if axis == axis_at else 1 for axis in range(len(extent))])
    return level


def noise(key, extent, scale, most, cuts=(), kind=jnp.bfloat16):
    values = scale * jax.random.normal(key, extent, jnp.float32)
    if cuts:
        values = values * shard_levels(key, extent, cuts, -0.22, 0.18)
    return jnp.clip(values, -most, most).astype(kind)


def setup_inputs(seed: int = 0) -> dict:
    seeds = jax.random.split(jax.random.key(seed), 25)
    return {
        "tokens": noise(seeds[0], (TOKENS, D), 1.0, 6.0, ((0, 32),)),
        "cotangent": draw_cotangent(jax.random.fold_in(seeds[24], 71), 0),
        "lengths": draw_lengths(jax.random.fold_in(seeds[24], 71), 0),
        "attend": noise(seeds[3], (3, D, D), D ** -0.5, 0.1875, ((1, 8), (2, 4)), jnp.float32),
        "mixing": noise(seeds[4], (D, D), D ** -0.5, 0.1875, ((0, 4), (1, 8)), jnp.float32),
        "expand": noise(seeds[5], (D, FF), D ** -0.5, 0.1875, ((0, 8), (1, 4)), jnp.float32),
        "contract": noise(seeds[6], (FF, D), FF ** -0.5, 0.09375, ((0, 4), (1, 8)), jnp.float32),
        "outer_norms": draw_outer_norms(jax.random.fold_in(seeds[24], 71), 0),
        "head_norms": draw_head_norms(jax.random.fold_in(seeds[24], 71), 0),
        "unit_norms": draw_unit_norms(jax.random.fold_in(seeds[24], 71), 0),
        "attend_moment": noise(seeds[10], (3, D, D), (3e-5), 0.00018310547, ((1, 8), (2, 4)), jnp.float32),
        "mixing_moment": noise(seeds[11], (D, D), (3e-5), 0.00018310547, ((0, 4), (1, 8)), jnp.float32),
        "expand_moment": noise(seeds[12], (D, FF), (3e-5), 0.00018310547, ((0, 8), (1, 4)), jnp.float32),
        "contract_moment": noise(seeds[13], (FF, D), (3e-5), 0.00018310547, ((0, 4), (1, 8)), jnp.float32),
        "outer_moment": noise(seeds[14], (4, D), (3e-5), 0.00018310547, ((1, 32),), jnp.float32),
        "head_moment": noise(seeds[15], (2, D), (3e-5), 0.00018310547, ((1, 32),), jnp.float32),
        "unit_moment": noise(seeds[16], (2, FF), (3e-5), 0.00018310547, ((1, 32),), jnp.float32),
        "attend_square": jnp.clip(jnp.exp(math.log(1.5999999547489097e-08) - 2.7725887 * jax.random.uniform(seeds[17], (3, D, D), jnp.float32) ** shard_levels(seeds[17], (3, D, D), ((1, 8), (2, 4)), -0.2, 0.2)), 9.999999717180685e-10, 1.5999999547489097e-08),
        "mixing_square": jnp.clip(jnp.exp(math.log(1.5999999547489097e-08) - 2.7725887 * jax.random.uniform(seeds[18], (D, D), jnp.float32) ** shard_levels(seeds[18], (D, D), ((0, 4), (1, 8)), -0.2, 0.2)), 9.999999717180685e-10, 1.5999999547489097e-08),
        "expand_square": jnp.clip(jnp.exp(math.log(1.5999999547489097e-08) - 2.7725887 * jax.random.uniform(seeds[19], (D, FF), jnp.float32) ** shard_levels(seeds[19], (D, FF), ((0, 8), (1, 4)), -0.2, 0.2)), 9.999999717180685e-10, 1.5999999547489097e-08),
        "contract_square": jnp.clip(jnp.exp(math.log(1.5999999547489097e-08) - 2.7725887 * jax.random.uniform(seeds[20], (FF, D), jnp.float32) ** shard_levels(seeds[20], (FF, D), ((0, 4), (1, 8)), -0.2, 0.2)), 9.999999717180685e-10, 1.5999999547489097e-08),
        "outer_square": jnp.clip(jnp.exp(math.log(1.5999999547489097e-08) - 2.7725887 * jax.random.uniform(seeds[21], (4, D), jnp.float32) ** shard_levels(seeds[21], (4, D), ((1, 32),), -0.2, 0.2)), 9.999999717180685e-10, 1.5999999547489097e-08),
        "head_square": jnp.clip(jnp.exp(math.log(1.5999999547489097e-08) - 2.7725887 * jax.random.uniform(seeds[22], (2, D), jnp.float32) ** shard_levels(seeds[22], (2, D), ((1, 32),), -0.2, 0.2)), 9.999999717180685e-10, 1.5999999547489097e-08),
        "unit_square": jnp.clip(jnp.exp(math.log(1.5999999547489097e-08) - 2.7725887 * jax.random.uniform(seeds[23], (2, FF), jnp.float32) ** shard_levels(seeds[23], (2, FF), ((1, 32),), -0.2, 0.2)), 9.999999717180685e-10, 1.5999999547489097e-08),
    }


@jax.custom_vjp
def low(v):
    return lax.optimization_barrier(v.astype(jnp.bfloat16)).astype(jnp.float32)

@jax.custom_vjp
def low_back(v):
    return v

def low_keep(v):
    return (low(v), None)

def low_pass(kept, grad):
    return (grad,)

def back_keep(v):
    return (v, None)

def back_low(kept, grad):
    return (low(grad),)
low.defvjp(low_keep, low_pass)
low_back.defvjp(back_keep, back_low)
PRECISE = lax.Precision.HIGHEST
NORM_EPS = 1e-05
MASKED = -1e+30
RATE = 0.02
BETA_ONE = 0.9
BETA_TWO = 0.95
ADAM_EPS = 1e-08
DECAY = 0.1
MAX_NORM = 1.0

def layer_norm(value, gain, bias):
    mean = lax.optimization_barrier(jnp.mean(value, axis=-1, keepdims=True))
    centered = value - mean
    variance = lax.optimization_barrier(jnp.mean(centered * centered, axis=-1, keepdims=True))
    return centered * lax.rsqrt(variance + NORM_EPS) * gain + bias

def segments_of(lengths):
    ends = jnp.cumsum(lengths, axis=1)
    places = jnp.arange(TOK_DEV, dtype=jnp.int32)
    return lax.optimization_barrier(jnp.sum((places[None, :, None] >= ends[:, None, :]).astype(jnp.int32), axis=2))

def group_attention(query, keys, values, segment):
    scores = jnp.einsum('qhd,khd->hqk', query, keys, precision=PRECISE) * HD ** (-0.5)
    scores = low_back(scores)
    allowed = segment[:, None] == segment[None, :]
    scores = jnp.where(allowed[None], scores, MASKED)
    highest = lax.optimization_barrier(jnp.max(scores, axis=2, keepdims=True))
    weights = jnp.exp(scores - highest)
    probs = weights / lax.optimization_barrier(jnp.sum(weights, axis=2, keepdims=True))
    return jnp.einsum('hqk,khd->qhd', low(probs), values, precision=PRECISE)

def forward(inputs, attend, mixing, expand, contract, outer, heads_gain, units_gain, segments):
    checked = jax.checkpoint(group_attention)
    normed_in = low(layer_norm(inputs, outer[0], outer[1]))
    projected = jnp.einsum('td,cde->cte', normed_in, low(attend), precision=PRECISE)
    projected = low(low_back(projected))
    shaped = projected.reshape(3, GROUPS, TOK_DEV, HEADS, HD)
    attended = lax.map(lambda parts: checked(parts[0], parts[1], parts[2], parts[3]), (shaped[0], shaped[1], shaped[2], segments))
    attended = low(low_back(attended.reshape(TOKENS, D)))
    head_normed = low(layer_norm(attended, heads_gain[0], heads_gain[1]))
    branch = low_back(jnp.dot(head_normed, low(mixing), precision=PRECISE))
    middle = inputs + branch
    mid_normed = low(layer_norm(middle, outer[2], outer[3]))
    widened = low_back(jnp.dot(mid_normed, low(expand), precision=PRECISE))
    activated = jax.nn.gelu(widened, approximate=False)
    unit_normed = low(layer_norm(activated, units_gain[0], units_gain[1]))
    feed = low_back(jnp.dot(unit_normed, low(contract), precision=PRECISE))
    return middle + feed

def adamw(param, grad, moment, square, clip, fix_one, fix_two):
    clipped = grad * clip
    moment_new = BETA_ONE * moment + (1.0 - BETA_ONE) * clipped
    square_new = BETA_TWO * square + (1.0 - BETA_TWO) * clipped * clipped
    change = -RATE * (moment_new / fix_one / (jnp.sqrt(square_new / fix_two) + ADAM_EPS) + DECAY * param)
    return (grad, moment_new, square_new, change)

def reference(tokens, cotangent, lengths, attend, mixing, expand, contract, outer_norms, head_norms, unit_norms, attend_moment, mixing_moment, expand_moment, contract_moment, outer_moment, head_moment, unit_moment, attend_square, mixing_square, expand_square, contract_square, outer_square, head_square, unit_square):
    segments = segments_of(lengths)
    live = (segments < SEQS).astype(jnp.float32).reshape(TOKENS, 1)

    def run(inputs, attend_w, mixing_w, expand_w, contract_w, outer_w, head_w, unit_w):
        return forward(inputs, attend_w, mixing_w, expand_w, contract_w, outer_w, head_w, unit_w, segments)
    result, pull = jax.vjp(run, tokens.astype(jnp.float32), attend, mixing, expand, contract, outer_norms, head_norms, unit_norms)
    grads = pull(cotangent.astype(jnp.float32) * live)
    total = jnp.float32(0.0)
    for grad in grads[1:]:
        total = total + jnp.sum(grad * grad)
    norm = jnp.sqrt(total)
    clip = jnp.minimum(1.0, MAX_NORM / (norm + 1e-06))
    count = jnp.float32(ADAM_STEP)
    fix_one = 1.0 - jnp.power(jnp.float32(BETA_ONE), count)
    fix_two = 1.0 - jnp.power(jnp.float32(BETA_TWO), count)
    first = adamw(attend, grads[1], attend_moment, attend_square, clip, fix_one, fix_two)
    second = adamw(mixing, grads[2], mixing_moment, mixing_square, clip, fix_one, fix_two)
    third = adamw(expand, grads[3], expand_moment, expand_square, clip, fix_one, fix_two)
    fourth = adamw(contract, grads[4], contract_moment, contract_square, clip, fix_one, fix_two)
    fifth = adamw(outer_norms, grads[5], outer_moment, outer_square, clip, fix_one, fix_two)
    sixth = adamw(head_norms, grads[6], head_moment, head_square, clip, fix_one, fix_two)
    seventh = adamw(unit_norms, grads[7], unit_moment, unit_square, clip, fix_one, fix_two)
    return (result.astype(jnp.bfloat16), grads[0], norm, first[0], first[1], first[2], first[3], second[0], second[1], second[2], second[3], third[0], third[1], third[2], third[3], fourth[0], fourth[1], fourth[2], fourth[3], fifth[0], fifth[1], fifth[2], fifth[3], sixth[0], sixth[1], sixth[2], sixth[3], seventh[0], seventh[1], seventh[2], seventh[3])
```

```python
from functools import partial

import jax
import jax.numpy as jnp
from jax import lax
from jax.experimental import pallas as pl
from jax.experimental.pallas import tpu as pltpu
from jax.sharding import PartitionSpec as P

D = 1024
HD = 64
FF = 4096
ADAM_STEP = 10

NORM_EPS = 1e-05
MASKED = -1e30
RATE = 0.02
BETA_ONE = 0.9
BETA_TWO = 0.95
ADAM_EPS = 1e-08
DECAY = 0.1
MAX_NORM = 1.0

BF = jnp.bfloat16
F32 = jnp.float32
ALL = ("dp", "mp")


def swap(value, bit):
    count = lax.axis_size("mp")
    return lax.ppermute(value, "mp", [(i, i ^ bit) for i in range(count)])


def mp_bits():
    count = lax.axis_size("mp")
    return [1 << b for b in range(count.bit_length() - 1)]


def gather_blocks(own):
    blocks = {0: own}
    for bit in reversed(mp_bits()):
        for r in list(blocks):
            blocks[r | bit] = swap(blocks[r], bit)
    return [blocks[r] for r in range(len(blocks))]


def sum_blocks(blocks):
    current = dict(enumerate(blocks))
    for bit in mp_bits():
        for r in [r for r in current if r & bit]:
            received = swap(current.pop(r).astype(BF), bit)
            current[r ^ bit] = current[r ^ bit].astype(F32) + received.astype(F32)
    return current[0]


def token_totals(first, second):
    count = lax.axis_size("mp")
    both = jnp.stack([first, second]).reshape(2, count, -1)
    for bit in mp_bits():
        received = swap(both, bit)
        both = both + jnp.stack([received[:, r ^ bit] for r in range(count)], axis=1)
    flat = both.reshape(2, -1)
    return flat[0], flat[1]


def exchange_all(value):
    return lax.all_to_all(value, ALL, 0, 0, tiled=True)


def norm_rows(value):
    mean = jnp.mean(value, axis=-1, keepdims=True)
    centered = value - mean
    variance = jnp.mean(centered * centered, axis=-1, keepdims=True)
    factor = lax.rsqrt(variance + NORM_EPS)
    return centered * factor, factor


def norm_back(grad, normed, factor, gain):
    weighted = grad * gain
    result = factor * (
        weighted
        - jnp.mean(weighted, axis=-1, keepdims=True)
        - normed * jnp.mean(weighted * normed, axis=-1, keepdims=True)
    )
    return result, jnp.sum(grad * normed, axis=0), jnp.sum(grad, axis=0)


def split_norm(value, width):
    first, second = token_totals(jnp.sum(value, axis=1), jnp.sum(value * value, axis=1))
    mean = first / width
    variance = second / width - mean * mean
    factor = lax.rsqrt(variance + NORM_EPS)
    return (value - mean[:, None]) * factor[:, None], factor


def split_norm_back(grad, normed, factor, gain, width):
    weighted = grad * gain
    first, second = token_totals(jnp.sum(weighted, axis=1), jnp.sum(weighted * normed, axis=1))
    result = factor[:, None] * (
        weighted - first[:, None] / width - normed * (second[:, None] / width)
    )
    return (result, jnp.sum(grad * normed, axis=0), jnp.sum(grad, axis=0))


def dot(left, right, left_dim, right_dim):
    return lax.dot_general(
        left, right, (((left_dim,), (right_dim,)), ((), ())), preferred_element_type=F32
    )


def segments_at(rows, table_ref, count):
    slots = rows ^ table_ref[count]
    end = jnp.int32(0)
    segment = jnp.zeros(rows.shape, jnp.int32)
    for i in range(count):
        end = end + table_ref[i]
        segment = segment + (slots >= end).astype(jnp.int32)
    return segment


def forward_kernel(table_ref, q_ref, k_ref, v_ref, o_ref, log_ref, *, block, heads, count):
    length, width = k_ref.shape
    start = pl.program_id(0) * block
    rows = start + lax.broadcasted_iota(jnp.int32, (block, 1), 0)
    columns = lax.broadcasted_iota(jnp.int32, (1, length), 1)
    allowed = segments_at(rows, table_ref, count) == segments_at(columns, table_ref, count)
    lane = lax.broadcasted_iota(jnp.int32, (1, width), 1) // HD
    query = q_ref[...] * BF(HD**-0.5)
    keys = k_ref[...]
    values = v_ref[...]
    out = jnp.zeros((block, width), F32)
    logs = []
    for h in range(heads):
        one = jnp.where(lane == h, query, jnp.zeros_like(query))
        scores = jnp.where(allowed, dot(one, keys, 1, 1), MASKED)
        highest = jnp.max(scores, axis=1, keepdims=True)
        weights = jnp.exp(scores - highest)
        total = jnp.sum(weights, axis=1, keepdims=True)
        mixed = dot(weights.astype(BF), values, 1, 0)
        out = jnp.where(lane == h, mixed * (1.0 / total), out)
        logs.append(highest + jnp.log(total))
    o_ref[...] = out.astype(BF)
    spread = 128 // heads
    logs = jnp.concatenate([jnp.broadcast_to(x, (block, spread)) for x in logs], axis=1)
    turned = jnp.transpose(logs)
    log_ref[...] = jnp.zeros_like(log_ref)
    for h in range(heads):
        log_ref[h : h + 1, :] = turned[h * spread : h * spread + 1, :]


def attention_forward(projected, table):
    length, width = projected.shape[0], projected.shape[1] // 3
    heads = width // HD
    block = min(512, length)
    return pl.pallas_call(
        partial(forward_kernel, block=block, heads=heads, count=table.shape[0] - 1),
        grid_spec=pltpu.PrefetchScalarGridSpec(
            num_scalar_prefetch=1,
            grid=(length // block,),
            in_specs=[
                pl.BlockSpec((block, width), lambda i, t: (i, 0)),
                pl.BlockSpec((length, width), lambda i, t: (0, 1)),
                pl.BlockSpec((length, width), lambda i, t: (0, 2)),
            ],
            out_specs=[
                pl.BlockSpec((block, width), lambda i, t: (i, 0)),
                pl.BlockSpec((8, block), lambda i, t: (0, i)),
            ],
        ),
        out_shape=[
            jax.ShapeDtypeStruct((length, width), BF),
            jax.ShapeDtypeStruct((8, length), F32),
        ],
        cost_estimate=pl.CostEstimate(
            flops=16 * length * length * width,
            transcendentals=heads * length * length,
            bytes_accessed=8 * length * width,
        ),
        compiler_params=pltpu.CompilerParams(vmem_limit_bytes=48 << 20),
        name="attention_forward",
    )(table, projected, projected, projected)


def backward_kernel(
    table_ref, q_ref, k_ref, v_ref, g_ref, o_ref, log_ref, out_q, out_k, out_v, sums, dots, *, block, heads, count
):
    length, width = q_ref.shape
    step = pl.program_id(0)
    lane = lax.broadcasted_iota(jnp.int32, (1, width), 1) // HD
    grad = g_ref[...]

    @pl.when(step == 0)
    def _():
        sums[...] = jnp.zeros_like(sums)
        picks = (
            lax.broadcasted_iota(jnp.int32, (8, width), 0)
            == lax.broadcasted_iota(jnp.int32, (8, width), 1) // HD
        ).astype(F32)
        products = grad.astype(F32) * o_ref[...].astype(F32)
        dots[...] = lax.dot_general(
            picks,
            products,
            (((1,), (1,)), ((), ())),
            precision=lax.Precision.HIGHEST,
            preferred_element_type=F32,
        )

    rows = step * block + lax.broadcasted_iota(jnp.int32, (block, 1), 0)
    columns = lax.broadcasted_iota(jnp.int32, (1, length), 1)
    allowed = segments_at(rows, table_ref, count) == segments_at(columns, table_ref, count)
    query = q_ref[...] * BF(HD**-0.5)
    keys = k_ref[...]
    values = v_ref[...]
    none = jnp.zeros_like(keys)
    key_back = jnp.zeros((block, width), F32)
    value_back = jnp.zeros((block, width), F32)
    for h in range(heads):
        key = jnp.where(lane == h, keys, none)
        value = jnp.where(lane == h, values, none)
        scores = jnp.where(allowed, dot(key, query, 1, 1), MASKED)
        probs = jnp.exp(scores - log_ref[h : h + 1, :])
        probs_back = dot(value, grad, 1, 1)
        score_back = (probs * (probs_back - dots[h : h + 1, :])).astype(BF)
        value_back = jnp.where(lane == h, dot(probs.astype(BF), grad, 1, 0), value_back)
        key_back = jnp.where(lane == h, dot(score_back, query, 1, 0), key_back)
        sums[...] += dot(score_back, key, 0, 0)
    out_k[...] = key_back.astype(BF)
    out_v[...] = value_back.astype(BF)

    @pl.when(step == pl.num_programs(0) - 1)
    def _():
        out_q[...] = (sums[...] * HD**-0.5).astype(BF)


def attention_backward(projected, table, grad, attended, logs):
    length, width = grad.shape
    heads = width // HD
    block = min(512, length)
    whole = pl.BlockSpec((length, width), lambda i, t: (0, 0))
    return pl.pallas_call(
        partial(backward_kernel, block=block, heads=heads, count=table.shape[0] - 1),
        grid_spec=pltpu.PrefetchScalarGridSpec(
            num_scalar_prefetch=1,
            grid=(length // block,),
            in_specs=[
                whole,
                pl.BlockSpec((block, width), lambda i, t: (i, 1)),
                pl.BlockSpec((block, width), lambda i, t: (i, 2)),
                whole,
                whole,
                pl.BlockSpec((8, length), lambda i, t: (0, 0)),
            ],
            out_specs=[
                whole,
                pl.BlockSpec((block, width), lambda i, t: (i, 0)),
                pl.BlockSpec((block, width), lambda i, t: (i, 0)),
            ],
            scratch_shapes=[pltpu.VMEM((length, width), F32), pltpu.VMEM((8, length), F32)],
        ),
        out_shape=[jax.ShapeDtypeStruct((length, width), BF)] * 3,
        cost_estimate=pl.CostEstimate(
            flops=40 * length * length * width,
            transcendentals=heads * length * length,
            bytes_accessed=16 * length * width,
        ),
        compiler_params=pltpu.CompilerParams(vmem_limit_bytes=56 << 20),
        name="attention_backward",
    )(table, projected, projected, projected, grad, attended, logs)


def adamw(param, grad, moment, square, clip, fix_one, fix_two):
    clipped = grad * clip
    moment_new = BETA_ONE * moment + (1.0 - BETA_ONE) * clipped
    square_new = BETA_TWO * square + (1.0 - BETA_TWO) * clipped * clipped
    change = -RATE * (
        moment_new / fix_one / (jnp.sqrt(square_new / fix_two) + ADAM_EPS) + DECAY * param
    )
    return (moment_new, square_new, change)


def local(
    tokens,
    cotangent,
    lengths,
    attend,
    mixing,
    expand,
    contract,
    outer_norms,
    head_norms,
    unit_norms,
    attend_moment,
    mixing_moment,
    expand_moment,
    contract_moment,
    outer_moment,
    head_moment,
    unit_moment,
    attend_square,
    mixing_square,
    expand_square,
    contract_square,
    outer_square,
    head_square,
    unit_square,
):
    height = tokens.shape[0]
    shard_count = lax.axis_size("mp")
    device_count = lax.axis_size("dp") * shard_count
    length_all = height * shard_count
    place = lax.axis_index("mp")
    sequences = lengths.shape[1]
    head_width = attend.shape[2]
    unit_width = expand.shape[1]
    shard = attend.shape[1]

    work_in = lax.all_gather(
        attend.astype(BF).transpose(1, 0, 2).reshape(shard, 3 * head_width), "dp", axis=0, tiled=True
    )
    work_mix = lax.all_gather(mixing.astype(BF).T, "dp", axis=0, tiled=True)
    work_exp = lax.all_gather(expand.astype(BF), "dp", axis=0, tiled=True)
    work_con = lax.all_gather(contract.astype(BF).T, "dp", axis=0, tiled=True)

    sizes = [x.size for x in (outer_norms, head_norms, unit_norms)]
    packed = jnp.concatenate([outer_norms.reshape(-1), head_norms.reshape(-1), unit_norms.reshape(-1)])
    tables = exchange_all(jnp.broadcast_to(packed[None], (device_count, packed.shape[0])))

    def unpack(start, rows):
        part = tables[:, start : start + sizes_at(start)].reshape(device_count, rows, -1)
        return part.transpose(1, 0, 2).reshape(rows, -1)

    def sizes_at(start):
        return {0: sizes[0], sizes[0]: sizes[1], sizes[0] + sizes[1]: sizes[2]}[start]

    outer = unpack(0, 4)
    head_gain = unpack(sizes[0], 2)
    unit_gain = unpack(sizes[0] + sizes[1], 2)
    head_local = lax.dynamic_slice_in_dim(head_gain, place * head_width, head_width, 1)
    unit_local = lax.dynamic_slice_in_dim(unit_gain, place * unit_width, unit_width, 1)

    table = jnp.concatenate([lengths[0], (place * height)[None].astype(jnp.int32)])
    slots = jnp.arange(length_all, dtype=jnp.int32) ^ (place * height)
    live_all = slots < jnp.sum(lengths)
    live = live_all[:height].astype(F32)[:, None]

    token_blocks = gather_blocks(tokens)
    tokens_all = jnp.concatenate(token_blocks, axis=0)
    normed_all = (norm_rows(tokens_all.astype(F32))[0] * outer[0] + outer[1]).astype(BF)
    projected = jnp.dot(normed_all, work_in, preferred_element_type=F32).astype(BF)

    back_raw = jnp.concatenate(gather_blocks(cotangent), axis=0)
    back_all = jnp.where(live_all[:, None], back_raw, jnp.zeros_like(back_raw))

    attended, logs = attention_forward(projected, table)
    head_normed, head_factor = split_norm(attended.astype(F32), D)
    mixed_in = (head_normed * head_local[0] + head_local[1]).astype(BF)

    def row_blocks(value):
        return [value[r * height : (r + 1) * height] for r in range(shard_count)]

    branch = sum_blocks(row_blocks(dot(mixed_in, work_mix, 1, 1).astype(BF)))
    inputs = tokens.astype(F32)
    middle = inputs + branch
    mid_normed, mid_factor = norm_rows(middle)
    mid_own = (mid_normed * outer[2] + outer[3]).astype(BF)
    mid_all = jnp.concatenate(gather_blocks(mid_own), axis=0)

    widened = jnp.dot(mid_all, work_exp, preferred_element_type=F32)
    activated, gelu_pull = jax.vjp(partial(jax.nn.gelu, approximate=False), widened)
    unit_normed, unit_factor = split_norm(activated, FF)
    unit_low = (unit_normed * unit_local[0] + unit_local[1]).astype(BF)
    feed = sum_blocks(row_blocks(dot(unit_low, work_con, 1, 1).astype(BF)))
    result = middle + feed

    back_out = cotangent.astype(F32) * live
    contract_back = dot(back_all, unit_low, 0, 0)
    unit_in = dot(back_all, work_con, 1, 0)
    unit_back, unit_gain_back, unit_bias_back = split_norm_back(
        unit_in, unit_normed, unit_factor, unit_local[0], FF
    )
    (widened_back,) = gelu_pull(unit_back)
    widened_low = widened_back.astype(BF)
    mid_in = sum_blocks(row_blocks(dot(widened_low, work_exp, 1, 1).astype(BF)))
    expand_back = dot(mid_all, widened_low, 0, 0)
    middle_part, gain_two, bias_two = norm_back(mid_in, mid_normed, mid_factor, outer[2])
    middle_back = back_out + middle_part
    middle_all = jnp.concatenate(gather_blocks(middle_back.astype(BF)), axis=0)
    mixed_back = dot(middle_all, work_mix, 1, 0)
    mixing_back = dot(middle_all, mixed_in, 0, 0)
    heads_back, head_gain_back, head_bias_back = split_norm_back(
        mixed_back, head_normed, head_factor, head_local[0], D
    )
    attended_back = heads_back.astype(BF)
    query_back, key_back, value_back = attention_backward(
        projected, table, attended_back, attended, logs
    )
    projected_back = jnp.concatenate([query_back, key_back, value_back], axis=1)
    attend_back = dot(normed_all, projected_back, 0, 0)
    normed_back = sum_blocks(row_blocks(dot(projected_back, work_in, 1, 1).astype(BF)))
    first_normed, first_factor = norm_rows(inputs)
    input_part, gain_one, bias_one = norm_back(normed_back, first_normed, first_factor, outer[0])
    input_grad = middle_back + input_part

    def scatter(value):
        return lax.psum_scatter(value.astype(BF), "dp", scatter_dimension=0, tiled=True).astype(F32)

    contract_grad = scatter(contract_back).T
    expand_grad = scatter(expand_back)
    mixing_grad = scatter(mixing_back).T
    attend_grad = scatter(attend_back).reshape(shard, 3, head_width).transpose(1, 0, 2)

    def widen(parts, width, full):
        return lax.dynamic_update_slice_in_dim(
            jnp.zeros((2, full), F32), jnp.stack(parts), place * width, 1
        )

    def for_owners(value):
        return value.reshape(value.shape[0], device_count, -1).transpose(1, 0, 2).reshape(device_count, -1)

    terms = jnp.concatenate(
        [
            for_owners(jnp.stack([gain_one, bias_one, gain_two, bias_two])),
            for_owners(widen([head_gain_back, head_bias_back], head_width, D)),
            for_owners(widen([unit_gain_back, unit_bias_back], unit_width, FF)),
        ],
        axis=1,
    )
    sums = jnp.sum(exchange_all(terms), axis=0)
    outer_grad = sums[: sizes[0]].reshape(outer_norms.shape)
    head_grad = sums[sizes[0] : sizes[0] + sizes[1]].reshape(head_norms.shape)
    unit_grad = sums[sizes[0] + sizes[1] :].reshape(unit_norms.shape)

    gradients = (attend_grad, mixing_grad, expand_grad, contract_grad, outer_grad, head_grad, unit_grad)
    local_squares = jnp.float32(0.0)
    for gradient in gradients:
        local_squares = local_squares + jnp.sum(gradient * gradient)
    all_squares = exchange_all(jnp.broadcast_to(local_squares, (device_count, 128)))
    norm = jnp.sqrt(jnp.sum(all_squares[:, 0]))
    clip = jnp.minimum(1.0, MAX_NORM / (norm + 1e-06))
    count_steps = jnp.float32(ADAM_STEP)
    fix_one = 1.0 - jnp.power(jnp.float32(BETA_ONE), count_steps)
    fix_two = 1.0 - jnp.power(jnp.float32(BETA_TWO), count_steps)
    params = (attend, mixing, expand, contract, outer_norms, head_norms, unit_norms)
    moments = (
        attend_moment,
        mixing_moment,
        expand_moment,
        contract_moment,
        outer_moment,
        head_moment,
        unit_moment,
    )
    squares = (
        attend_square,
        mixing_square,
        expand_square,
        contract_square,
        outer_square,
        head_square,
        unit_square,
    )
    results = [result.astype(BF), input_grad, norm]
    for param, gradient, moment, square in zip(params, gradients, moments, squares):
        results.append(gradient)
        results.extend(adamw(param, gradient, moment, square, clip, fix_one, fix_two))
    return tuple(results)


def solution(mesh):
    rows = P(ALL, None)
    norms = P(None, ALL)
    weights = (P(None, "dp", "mp"), P("mp", "dp"), P("dp", "mp"), P("mp", "dp"))
    states = weights + (norms,) * 3
    outs = (rows, rows, P())
    for spec in states:
        outs = outs + (spec,) * 4
    return jax.shard_map(
        local,
        mesh=mesh,
        in_specs=(rows, rows, P("dp", None)) + states * 3,
        out_specs=outs,
        check_vma=False,
    )
```

```python
from functools import partial

import jax
import jax.numpy as jnp
from jax import lax
from jax.experimental import pallas as pl
from jax.experimental.pallas import tpu as pltpu
from jax.sharding import PartitionSpec as P

D = 1024
HD = 64
FF = 4096
ADAM_STEP = 10

NORM_EPS = 1e-05
MASKED = -1e30
RATE = 0.02
BETA_ONE = 0.9
BETA_TWO = 0.95
ADAM_EPS = 1e-08
DECAY = 0.1
MAX_NORM = 1.0

BF = jnp.bfloat16
F32 = jnp.float32
ALL = ("dp", "mp")


def swap(value, bit):
    count = lax.axis_size("mp")
    return lax.ppermute(value, "mp", [(i, i ^ bit) for i in range(count)])


def mp_bits():
    count = lax.axis_size("mp")
    return [1 << b for b in range(count.bit_length() - 1)]


def after(values, others):
    values, _ = lax.optimization_barrier((tuple(values), tuple(others)))
    return list(values)


def gather_near(own):
    even = {0: own}
    for bit in reversed(mp_bits()[1:]):
        for r in list(even):
            even[r | bit] = swap(even[r], bit)
    return [own, swap(own, 1)], [even[r] for r in range(2, 2 * len(even), 2)]


def gather_far(even):
    return [block for value in even for block in (value, swap(value, 1))]


def sum_chip(terms):
    return [
        terms[2 * i].astype(F32) + swap(terms[2 * i + 1], 1).astype(F32)
        for i in range(len(terms) // 2)
    ]


def sum_far(sums):
    even = {2 * i + 2: value for i, value in enumerate(sums)}
    arrived = []
    for bit in mp_bits()[1:]:
        for r in [r for r in even if r & bit]:
            received = swap(even.pop(r).astype(BF), bit)
            if r == bit:
                arrived.append(received)
            else:
                even[r ^ bit] = even[r ^ bit].astype(F32) + received.astype(F32)
    return arrived


def sum_near(terms, arrived):
    total = terms[0].astype(F32) + swap(terms[1], 1).astype(F32)
    for value in arrived:
        total = total + value.astype(F32)
    return total


def token_totals(values):
    count = lax.axis_size("mp")
    height = values.shape[1] // count
    for bit in mp_bits():
        received = swap(values, bit)
        parts = [received[:, (r ^ bit) * height : ((r ^ bit) + 1) * height] for r in range(count)]
        values = values + jnp.concatenate(parts, axis=1)
    return values


def exchange_all(value):
    return lax.all_to_all(value, ALL, 0, 0, tiled=True)


def dp_swap(value, bits):
    count = lax.axis_size("dp")
    return lax.ppermute(value, "dp", [(i, i ^ bits) for i in range(count)])


def place_kernel(table_ref, *refs):
    blocks, outs = refs[:8], refs[8:]
    rows = blocks[0].shape[0]
    for r, ref in enumerate(blocks):
        start = pl.multiple_of((table_ref[0] ^ r) * rows, rows)
        first = 0
        for out in outs:
            out[pl.ds(start, rows), :] = ref[:, first : first + out.shape[1]]
            first += out.shape[1]


def smem():
    return pl.BlockSpec(memory_space=pltpu.SMEM)


def vmem():
    return pl.BlockSpec(memory_space=pltpu.VMEM)


def gather_groups(shard):
    if lax.axis_size("dp") != 8:
        return [lax.all_gather(shard, "dp", axis=0, tiled=True)]
    return [shard] + [dp_swap(shard, bits) for bits in (2, 4, 6)]


def cross_groups(even, others):
    if len(even) == 1:
        return []
    first = dp_swap(even[0], 1)
    odd = [first, dp_swap(first, 2)]
    return odd + [dp_swap(value, 1) for value in after(even[2:], odd + even[1:2] + others)]


def place_groups(even, odd, widths):
    if len(even) == 1:
        return list(jnp.split(even[0], [sum(widths[: k + 1]) for k in range(len(widths) - 1)], axis=1))
    blocks = [block for both in zip(even, odd) for block in both]
    place = lax.axis_index("dp").astype(jnp.int32)[None]
    rows = even[0].shape[0]
    return pl.pallas_call(
        place_kernel,
        in_specs=[smem()] + [vmem()] * 8,
        out_specs=[vmem()] * len(widths),
        out_shape=[jax.ShapeDtypeStruct((8 * rows, width), even[0].dtype) for width in widths],
        cost_estimate=about(2),
        name="place_rows",
    )(place, *blocks)


def exchange_groups(value):
    return lax.all_to_all(value, "dp", 0, 0, tiled=True)


HINT = 4.0


def about(microseconds, hint=HINT):
    return pl.CostEstimate(
        flops=int(microseconds * hint * 1.15e9),
        transcendentals=0,
        bytes_accessed=int(microseconds * hint * 1e5),
    )


def dot(left, right, left_dim, right_dim):
    return lax.dot_general(
        left, right, (((left_dim,), (right_dim,)), ((), ())), preferred_element_type=F32
    )


def norm_rows(value):
    mean = jnp.mean(value, axis=-1, keepdims=True)
    centered = value - mean
    variance = jnp.mean(centered * centered, axis=-1, keepdims=True)
    factor = lax.rsqrt(variance + NORM_EPS)
    return centered * factor, factor


def norm_back(grad, normed, factor, gain):
    weighted = grad * gain
    result = factor * (
        weighted
        - jnp.mean(weighted, axis=-1, keepdims=True)
        - normed * jnp.mean(weighted * normed, axis=-1, keepdims=True)
    )
    return result, jnp.sum(grad * normed, axis=0), jnp.sum(grad, axis=0)


def as_rows(columns, count):
    rows = columns[0].shape[0]
    lane = lax.broadcasted_iota(jnp.int32, (rows, 128), 1)
    spread = jnp.zeros((rows, 128), F32)
    for i, column in enumerate(columns):
        spread = jnp.where(lane == i, column, spread)
    return jnp.transpose(spread)[:count]


def as_columns(values):
    count, rows = values.shape
    padded = jnp.concatenate([values, jnp.zeros((128 - count, rows), F32)], axis=0)
    turned = jnp.transpose(padded)
    return [turned[:, i : i + 1] for i in range(count)]


def fold(value):
    return jnp.sum(value.reshape(value.shape[0] // 8, 8, value.shape[1]), axis=0)


def moments(first, second, width):
    mean = first / width
    variance = second / width - mean * mean
    return mean, lax.rsqrt(variance + NORM_EPS)


class Rows:
    def __init__(self, blocks, height, step):
        self.blocks = blocks
        self.per = height // step
        self.step = step
        self.height = height
        self.grid = (len(blocks) * self.per,)

    def at(self, i):
        return i + self.blocks[0] * self.per

    def whole(self, width, column=0):
        return pl.BlockSpec((self.step, width), lambda i, *t: (self.at(i), column))

    def stats(self, count):
        return pl.BlockSpec((count, self.step), lambda i, *t: (0, self.at(i)))

    def pieces(self, width):
        per = self.per
        return [
            pl.BlockSpec(
                (self.step, width), lambda i, *t, first=k * per: (jnp.clip(i - first, 0, per - 1), 0)
            )
            for k in range(len(self.blocks))
        ]

    def load(self, refs, into):
        for k, ref in enumerate(refs):

            @pl.when(pl.program_id(0) // self.per == k)
            def _():
                into[...] = ref[...]

    def store(self, refs, value):
        for k, ref in enumerate(refs):

            @pl.when(pl.program_id(0) // self.per == k)
            def _():
                ref[...] = value


def fixed(shape, *index):
    index = index or (0,) * len(shape)
    return pl.BlockSpec(shape, lambda i, *t: index)


ANY = pl.BlockSpec(memory_space=pl.ANY)


def call(kernel, part, name, ins, in_specs, outs, out_specs, scratch=(), kept=None, table=None, cost=8, pieces=False):
    ins, in_specs = list(ins), list(in_specs)
    aliases = {}
    tables = [] if table is None else [table]
    if kept is not None:
        for k, value in enumerate(kept):
            aliases[len(tables) + len(ins)] = k
            ins.append(value)
            in_specs.append(ANY)
    dropped = 0 if kept is None else len(kept)
    used = len(tables) + len(ins) - dropped

    def body(*refs):
        kernel(*refs[:used], *refs[used + dropped :])

    hbm = len(outs) - len(part.blocks) if pieces else len(outs)
    return pl.pallas_call(
        body,
        grid_spec=pltpu.PrefetchScalarGridSpec(
            num_scalar_prefetch=len(tables),
            grid=part.grid,
            in_specs=in_specs,
            out_specs=list(out_specs),
            scratch_shapes=list(scratch),
        ),
        out_shape=[jax.ShapeDtypeStruct(*out) for out in outs[:hbm]]
        + [pltpu.HBM(*out) for out in outs[hbm:]],
        input_output_aliases=aliases,
        cost_estimate=about(cost * len(part.blocks) / 4),
        compiler_params=pltpu.CompilerParams(vmem_limit_bytes=50 << 20),
        name=name,
    )(*tables, *ins)


def project(part, blocks, work_in, outer):
    count, length = len(blocks), len(blocks) * part.height
    width = work_in.shape[1]

    def kernel(*refs):
        work_ref, gain_ref, normed_ref, out_ref, row = refs[count:]
        part.load(refs[:count], row)
        normed = norm_rows(row[...].astype(F32))[0]
        normed_ref[...] = normed.astype(BF)
        normed = (normed * gain_ref[0:1] + gain_ref[1:2]).astype(BF)
        out_ref[...] = dot(normed, work_ref[...], 1, 0).astype(BF)

    return call(
        kernel,
        part,
        "project",
        [*blocks, work_in, outer],
        [*part.pieces(D), fixed(work_in.shape), fixed(outer.shape)],
        [((length, D), BF), ((length, width), BF)],
        [part.whole(D), part.whole(width)],
        [pltpu.VMEM((part.step, D), BF)],
    )


def columns_of(table_ref, index, r, width):
    return pl.ds(pl.multiple_of((table_ref[index] ^ r) * width, width), width)


def head_norm(att_refs):
    parts = [ref[...].astype(F32) for ref in att_refs]
    mean = sum(jnp.sum(part, axis=1, keepdims=True) for part in parts) / D
    parts = [part - mean for part in parts]
    variance = sum(jnp.sum(part * part, axis=1, keepdims=True) for part in parts) / D
    factor = lax.rsqrt(variance + NORM_EPS)
    return [part * factor for part in parts], factor


def own_call(kernel, name, table, ins, in_specs, outs, out_specs, height, cost, scratch=()):
    return pl.pallas_call(
        kernel,
        grid_spec=pltpu.PrefetchScalarGridSpec(
            num_scalar_prefetch=1,
            grid=(height // OWN_STEP,),
            in_specs=in_specs,
            out_specs=out_specs,
            scratch_shapes=list(scratch),
        ),
        out_shape=[pltpu.HBM(*out) if out[1] == BF else jax.ShapeDtypeStruct(*out) for out in outs],
        cost_estimate=about(cost),
        compiler_params=pltpu.CompilerParams(vmem_limit_bytes=50 << 20),
        name=name,
    )(table, *ins)


OWN_STEP = 256


def own(width):
    return pl.BlockSpec((OWN_STEP, width), lambda i, t: (i, 0))


def mix_rows(table, sequences, blocks, mixes, gains, tokens, outer):
    count, (height, width) = len(blocks), blocks[0].shape

    def kernel(table_ref, *refs):
        att_refs, mix_refs = refs[:count], refs[count : 2 * count]
        gain_ref, token_ref, outer_ref, middle_ref, mid_ref, in_ref = refs[2 * count :]
        middle = token_ref[...].astype(F32)
        for r, normed in enumerate(head_norm(att_refs)[0]):
            columns = columns_of(table_ref, sequences + 1, r, width)
            low = (normed * gain_ref[0:1, columns] + gain_ref[1:2, columns]).astype(BF)
            in_ref[:, r * width : (r + 1) * width] = low
            middle = middle + dot(low, mix_refs[r][...], 1, 1)
        middle_ref[...] = middle
        mid_ref[...] = (norm_rows(middle)[0] * outer_ref[2:3] + outer_ref[3:4]).astype(BF)

    return own_call(
        kernel,
        "mix_rows",
        table,
        [*blocks, *mixes, gains, tokens, outer],
        [own(width)] * count + [fixed((D, width))] * count + [fixed((2, D)), own(D), fixed((4, D))],
        [((height, D), F32), ((height, D), BF), ((height, D), BF)],
        [own(D)] * 3,
        height,
        6,
    )


def mix_rows_back(table, sequences, terms, middle, cotangent, outer, blocks, mixes, gains):
    count, (height, width) = len(blocks), blocks[0].shape

    def kernel(table_ref, *refs):
        term_refs, refs = refs[: len(terms)], refs[len(terms) :]
        middle_ref, back_ref, outer_ref, gain_ref = refs[:4]
        att_refs, mix_refs = refs[4 : 4 + count], refs[4 + count : 4 + 2 * count]
        out_ref, low_ref, outer_sum, head_sum, *outs = refs[4 + 2 * count :]

        @pl.when(pl.program_id(0) == 0)
        def _():
            outer_sum[...] = jnp.zeros_like(outer_sum)
            head_sum[...] = jnp.zeros_like(head_sum)

        grad = sum(ref[...].astype(F32) for ref in term_refs)
        normed, factor = norm_rows(middle_ref[...])
        weighted = grad * outer_ref[2:3]
        first = jnp.mean(weighted, axis=1, keepdims=True)
        second = jnp.mean(weighted * normed, axis=1, keepdims=True)
        outer_sum[0:8] += fold(grad * normed)
        outer_sum[8:16] += fold(grad)
        rows = pl.program_id(0) * OWN_STEP + lax.broadcasted_iota(jnp.int32, (OWN_STEP, 1), 0)
        live = segments_at(rows, table_ref, sequences) < sequences
        back = jnp.where(live, back_ref[...].astype(F32), 0.0)
        back = back + factor * (weighted - first - normed * second)
        out_ref[...] = back
        low = back.astype(BF)
        low_ref[...] = low
        normed, factor = head_norm(att_refs)
        weighted = []
        first, second = 0.0, 0.0
        for r in range(count):
            columns = columns_of(table_ref, sequences + 1, r, width)
            grad = dot(low, mix_refs[r][...], 1, 0)
            head_sum[0:8, columns] += fold(grad * normed[r])
            head_sum[8:16, columns] += fold(grad)
            weighted.append(grad * gain_ref[0:1, columns])
            first = first + jnp.sum(weighted[r], axis=1, keepdims=True)
            second = second + jnp.sum(weighted[r] * normed[r], axis=1, keepdims=True)
        for r in range(count):
            value = factor * (weighted[r] - first / D - normed[r] * (second / D))
            outs[r][...] = value.astype(BF)

    return own_call(
        kernel,
        "mix_rows_back",
        table,
        [*terms, middle, cotangent, outer, gains, *blocks, *mixes],
        [own(D)] * (len(terms) + 2)
        + [fixed((4, D)), fixed((2, D))]
        + [own(width)] * count
        + [fixed((D, width))] * count,
        [((height, D), F32), ((height, D), BF), ((16, D), F32), ((16, D), F32)]
        + [((height, width), BF)] * count,
        [own(D), own(D), fixed((16, D)), fixed((16, D))] + [own(width)] * count,
        height,
        8,
    )


def mix_grads(low, mixed_in, count):
    height, width = low.shape[0], mixed_in.shape[1] // count
    block = 256

    def kernel(low_ref, in_ref, *outs):
        for r in range(count):
            outs[r][...] = dot(low_ref[...], in_ref[:, r * width : (r + 1) * width], 0, 0).astype(BF)

    return pl.pallas_call(
        kernel,
        grid=(D // block,),
        in_specs=[
            pl.BlockSpec((height, block), lambda i: (0, i)),
            pl.BlockSpec((height, D), lambda i: (0, 0)),
        ],
        out_specs=[pl.BlockSpec((block, width), lambda i: (i, 0))] * count,
        out_shape=[pltpu.HBM((D, width), BF)] * count,
        cost_estimate=about(4),
        compiler_params=pltpu.CompilerParams(vmem_limit_bytes=50 << 20),
        name="mix_grads",
    )(low, mixed_in)


def feed_back(part, blocks, table, sequences, weights):
    count, length = len(blocks), len(blocks) * part.height
    units = weights.shape[1] // 2

    def kernel(table_ref, *refs):
        work_ref, back_ref, out_ref, row = refs[count:]
        part.load(refs[:count], row)
        rows = pl.program_id(0) * part.step + lax.broadcasted_iota(jnp.int32, (part.step, 1), 0)
        live = segments_at(rows, table_ref, sequences) < sequences
        back = jnp.where(live, row[...].astype(F32), 0.0).astype(BF)
        back_ref[...] = back
        out_ref[...] = dot(back, work_ref[...], 1, 0).astype(BF)

    return call(
        kernel,
        part,
        "feed_back",
        [*blocks, weights],
        [*part.pieces(D), fixed((D, units), 0, 1)],
        [((length, D), BF), ((length, units), BF)],
        [part.whole(D), part.whole(units)],
        [pltpu.VMEM((part.step, D), BF)],
        table=table,
    )


def widen(part, blocks, weights, unit_in, gains, kept=None):
    count, (length, units) = len(blocks), unit_in.shape

    def kernel(*refs):
        work_ref, in_ref, gain_ref, mid_ref, act_ref, slope_ref, total_ref, row = refs[count:]
        part.load(refs[:count], row)
        mid_ref[...] = row[...]
        wide = dot(row[...], work_ref[...], 1, 0)
        share = 0.5 + 0.5 * lax.erf(wide * 0.7071067811865476)
        act = wide * share
        act_ref[...] = act
        slope_ref[...] = (share + wide * (0.3989422804014327 * jnp.exp(-0.5 * wide * wide))).astype(BF)
        weighted = in_ref[...].astype(F32) * gain_ref[0:1]
        values = (act, act * act, weighted, weighted * act)
        total_ref[...] = as_rows([jnp.sum(v, axis=1, keepdims=True) for v in values], 4)

    return call(
        kernel,
        part,
        "widen",
        [*blocks, weights, unit_in, gains],
        [*part.pieces(D), fixed((D, units), 0, 0), part.whole(units), fixed(gains.shape)],
        [((length, D), BF), ((length, units), F32), ((length, units), BF), ((4, length), F32)],
        [part.whole(D), part.whole(units), part.whole(units), part.stats(4)],
        [pltpu.VMEM((part.step, D), BF)],
        kept=kept,
    )


def narrow_back(part, act, slope, unit_in, totals, gains, weights, kept=None):
    length, units = act.shape

    def kernel(act_ref, slope_ref, in_ref, total_ref, gain_ref, work_ref, low_ref, wide_ref, sum_ref, *outs):
        first, second, third, fourth = as_columns(total_ref[...])
        mean, factor = moments(first, second, FF)
        normed = (act_ref[...] - mean) * factor
        low_ref[...] = (normed * gain_ref[0:1] + gain_ref[1:2]).astype(BF)
        grad = in_ref[...].astype(F32)
        inner = factor * (fourth - mean * third)
        back = factor * (grad * gain_ref[0:1] - third / FF - normed * (inner / FF))
        wide = (back * slope_ref[...].astype(F32)).astype(BF)
        wide_ref[...] = wide

        @pl.when(pl.program_id(0) == 0)
        def _():
            sum_ref[...] = jnp.zeros_like(sum_ref)

        sum_ref[0:8] += fold(grad * normed)
        sum_ref[8:16] += fold(grad)
        part.store(outs, dot(wide, work_ref[...], 1, 1).astype(BF))

    return call(
        kernel,
        part,
        "narrow_back",
        [act, slope, unit_in, totals, gains, weights],
        [part.whole(units)] * 3 + [part.stats(4), fixed(gains.shape), fixed((D, units), 0, 0)],
        [((length, units), BF)] * 2
        + [((16, units), F32)]
        + [((part.height, D), BF)] * len(part.blocks),
        [part.whole(units)] * 2 + [fixed((16, units))] + part.pieces(D),
        kept=kept,
        pieces=True,
    )


def weight_grad(left, right):
    length, block = left.shape[0], 256

    def kernel(left_ref, right_ref, out_ref):
        out_ref[...] = dot(left_ref[...], right_ref[...], 0, 0).astype(BF)

    return pl.pallas_call(
        kernel,
        grid=(left.shape[1] // block,),
        in_specs=[
            pl.BlockSpec((length, block), lambda i: (0, i)),
            pl.BlockSpec(right.shape, lambda i: (0, 0)),
        ],
        out_specs=pl.BlockSpec((block, right.shape[1]), lambda i: (i, 0)),
        out_shape=jax.ShapeDtypeStruct((left.shape[1], right.shape[1]), BF),
        cost_estimate=about(8),
        compiler_params=pltpu.CompilerParams(vmem_limit_bytes=50 << 20),
        name="weight_grad",
    )(left, right)


def feed_rows(part, low, weights):
    units = low.shape[1]

    def kernel(low_ref, work_ref, *outs):
        part.store(outs, dot(low_ref[...], work_ref[...], 1, 1).astype(BF))

    return call(
        kernel,
        part,
        "feed_rows",
        [low, weights],
        [part.whole(units), fixed((D, units), 0, 1)],
        [((part.height, D), BF)] * len(part.blocks),
        part.pieces(D),
        pieces=True,
    )


EXTRA = 16


def attend_rows(normed_all, back, extra=()):
    length, width = back.shape
    groups = lax.axis_size("dp")
    shard = D // groups
    more = extra[0].shape[1] if extra else 0

    def kernel(normed_ref, back_ref, *refs):
        out_ref, total_ref = refs[-2:]

        @pl.when(pl.program_id(0) == 0)
        def _():
            value = jnp.sum(fold(back_ref[...].astype(F32)), axis=0, keepdims=True)
            row = lax.broadcasted_iota(jnp.int32, (EXTRA, width), 0)
            total = jnp.zeros((EXTRA, width), F32)
            for k in range(3):
                piece = value.astype(BF).astype(F32)
                total = jnp.where(row == k, piece, total)
                value = value - piece
            total_ref[...] = total.astype(BF)

        start = pl.multiple_of(pl.program_id(0) * shard, shard)
        if shard % 128 == 0:
            normed = normed_ref[:, pl.ds(start, shard)]
        else:
            normed = normed_ref[...]
        out_ref[0, :shard, :width] = dot(normed, back_ref[...], 0, 0).astype(BF)
        out_ref[0, shard:, :width] = total_ref[...]
        if extra:
            value = sum(ref[...].astype(F32) for ref in refs[:-2])
            out_ref[0, :shard, width:] = value.astype(BF)
            out_ref[0, shard:, width:] = jnp.zeros((EXTRA, more), BF)

    if shard % 128 != 0:
        return attend_rows_narrow(normed_all, back, extra)
    return pl.pallas_call(
        kernel,
        grid=(groups,),
        in_specs=[
            pl.BlockSpec((length, D), lambda i: (0, 0)),
            pl.BlockSpec((length, width), lambda i: (0, 0)),
        ]
        + [pl.BlockSpec((shard, more), lambda i: (i, 0))] * len(extra),
        out_specs=pl.BlockSpec((1, shard + EXTRA, width + more), lambda i: (i, 0, 0)),
        out_shape=jax.ShapeDtypeStruct((groups, shard + EXTRA, width + more), BF),
        scratch_shapes=[pltpu.VMEM((EXTRA, width), BF)],
        cost_estimate=about(5),
        compiler_params=pltpu.CompilerParams(vmem_limit_bytes=50 << 20),
        name="attend_rows",
    )(normed_all, back, *extra)


def attend_rows_narrow(normed_all, back, extra):
    groups = lax.axis_size("dp")
    grads = dot(normed_all, back, 0, 0)
    total = jnp.sum(back.astype(F32), axis=0)
    addends = []
    for _ in range(3):
        addends.append(total.astype(BF))
        total = total - addends[-1].astype(F32)
    below = jnp.concatenate([jnp.stack(addends), jnp.zeros((EXTRA - 3, back.shape[1]), BF)], axis=0)
    if extra:
        grads = jnp.concatenate([grads, sum(value.astype(F32) for value in extra)], axis=1)
        below = jnp.concatenate([below, jnp.zeros((EXTRA, extra[0].shape[1]), BF)], axis=1)
    grads = grads.astype(BF).reshape(groups, D // groups, -1)
    below = jnp.broadcast_to(below[None], (groups,) + below.shape)
    return jnp.concatenate([grads, below], axis=1)


def attend_sums(piece, work, gains, width):
    groups, rows, columns = piece.shape
    shard = rows - EXTRA

    def kernel(piece_ref, work_ref, gain_ref, grad_ref, *outs):
        total = piece_ref[0].astype(F32)
        for k in range(1, groups):
            total = total + piece_ref[k].astype(F32)
        grad = total[:shard, :width]
        below = jnp.sum(total[shard:, :width], axis=0, keepdims=True)
        gain, bias = gain_ref[:, 0:1], gain_ref[:, 1:2]
        work = work_ref[...].astype(F32)
        grad_ref[...] = gain * grad + bias * below
        for k, value in enumerate((grad * work, below * work)):
            outs[0][:, k : k + 1] = jnp.sum(value, axis=1, keepdims=True)
        if columns > width:
            outs[1][...] = total[:shard, width:]

    outs = [((shard, width), F32), ((shard, 2), F32)]
    if columns > width:
        outs.append(((shard, columns - width), F32))
    return pl.pallas_call(
        kernel,
        in_specs=[vmem()] * 3,
        out_specs=[vmem()] * len(outs),
        out_shape=[jax.ShapeDtypeStruct(shape, kind) for shape, kind in outs],
        cost_estimate=about(2),
        compiler_params=pltpu.CompilerParams(vmem_limit_bytes=50 << 20),
        name="attend_sums",
    )(piece, work, gains)


def input_back(part, grads, work_in):
    width = grads[0].shape[1]

    def kernel(*refs):
        work_ref, outs = refs[len(grads)], refs[len(grads) + 1 :]
        term = dot(refs[0][...], work_ref[:, :width], 1, 1)
        for k in range(1, len(grads)):
            term = term + dot(refs[k][...], work_ref[:, k * width : (k + 1) * width], 1, 1)
        part.store(outs, term.astype(BF))

    return call(
        kernel,
        part,
        "input_back",
        [*grads, work_in],
        [part.whole(width)] * len(grads) + [fixed((D, len(grads) * width))],
        [((part.height, D), BF)] * len(part.blocks),
        part.pieces(D),
        pieces=True,
    )


def segments_at(rows, table_ref, count):
    slots = rows ^ table_ref[count]
    end = jnp.int32(0)
    segment = jnp.zeros(rows.shape, jnp.int32)
    for i in range(count):
        end = end + table_ref[i]
        segment = segment + (slots >= end).astype(jnp.int32)
    return segment


LANES = 128
PAIR = LANES // HD


def attention_forward(part, projected, table):
    length, width = projected.shape[0], projected.shape[1] // 3
    pairs = width // LANES
    block = part.height
    count = table.shape[0] - 2
    blocks = len(part.blocks)

    def kernel(table_ref, *refs):
        outs, log_ref, low = refs[3 * pairs : -2], refs[-2], refs[-1]
        start = pl.program_id(0) * block
        rows = start + lax.broadcasted_iota(jnp.int32, (block, 1), 0)
        columns = lax.broadcasted_iota(jnp.int32, (1, length), 1)
        allowed = segments_at(rows, table_ref, count) == segments_at(columns, table_ref, count)
        lane = lax.broadcasted_iota(jnp.int32, (1, LANES), 1) // HD
        for p in range(pairs):
            query = refs[3 * p][...] * BF(HD**-0.5)
            keys = refs[3 * p + 1][...]
            values = refs[3 * p + 2][...]
            out = jnp.zeros((block, LANES), F32)
            logs = []
            for h in range(PAIR):
                one = jnp.where(lane == h, query, jnp.zeros_like(query))
                scores = jnp.where(allowed, dot(one, keys, 1, 1), MASKED)
                highest = jnp.max(scores, axis=1, keepdims=True)
                weights = jnp.exp(scores - highest)
                total = jnp.sum(weights, axis=1, keepdims=True)
                mixed = dot(weights.astype(BF), values, 1, 0)
                out = jnp.where(lane == h, mixed * (1.0 / total), out)
                logs.append(highest + jnp.log(total))
            low[:, p * LANES : (p + 1) * LANES] = out.astype(BF)
            log_ref[8 * p : 8 * p + 8, :] = as_rows(logs, 8)
        part.store(outs, low[...])

    specs = []
    for p in range(pairs):
        specs.append(pl.BlockSpec((block, LANES), lambda i, t, p=p: (i, 3 * p)))
        specs.append(fixed((length, LANES), 0, 3 * p + 1))
        specs.append(fixed((length, LANES), 0, 3 * p + 2))
    *outs, logs = pl.pallas_call(
        kernel,
        grid_spec=pltpu.PrefetchScalarGridSpec(
            num_scalar_prefetch=1,
            grid=(blocks,),
            in_specs=specs,
            out_specs=part.pieces(width) + [pl.BlockSpec((8 * pairs, block), lambda i, t: (0, i))],
            scratch_shapes=[pltpu.VMEM((block, width), BF)],
        ),
        out_shape=[jax.ShapeDtypeStruct((block, width), BF)] * blocks
        + [jax.ShapeDtypeStruct((8 * pairs, length), F32)],
        cost_estimate=about(16 * pairs, 4.0),
        compiler_params=pltpu.CompilerParams(vmem_limit_bytes=48 << 20),
        name="attention_forward",
    )(table, *[projected] * (3 * pairs))
    return outs, logs


def backward_kernel(
    table_ref, q_ref, k_ref, v_ref, log_ref, *refs, block, count
):
    out, sums, dots, grads = refs[-4:]
    blocks = (len(refs) - 4) // 2
    length = q_ref.shape[0]
    step = pl.program_id(0)
    lane = lax.broadcasted_iota(jnp.int32, (1, LANES), 1) // HD

    @pl.when(step == 0)
    def _():
        sums[...] = jnp.zeros_like(sums)
        for r in range(blocks):
            low, attended = refs[r][...], refs[blocks + r][...]
            height = low.shape[0]
            grads[r * height : (r + 1) * height, :] = low
            products = low.astype(F32) * attended.astype(F32)
            dots[:, r * height : (r + 1) * height] = as_rows(
                [
                    jnp.sum(jnp.where(lane == h, products, 0.0), axis=1, keepdims=True)
                    for h in range(PAIR)
                ],
                8,
            )

    grad = grads[...]
    start = pl.multiple_of(step * block, block)
    rows = start + lax.broadcasted_iota(jnp.int32, (block, 1), 0)
    columns = lax.broadcasted_iota(jnp.int32, (1, length), 1)
    allowed = segments_at(rows, table_ref, count) == segments_at(columns, table_ref, count)
    query = q_ref[...] * BF(HD**-0.5)
    keys = k_ref[...]
    values = v_ref[...]
    none = jnp.zeros_like(keys)
    key_back = jnp.zeros((block, LANES), F32)
    value_back = jnp.zeros((block, LANES), F32)
    for h in range(PAIR):
        key = jnp.where(lane == h, keys, none)
        value = jnp.where(lane == h, values, none)
        scores = jnp.where(allowed, dot(key, query, 1, 1), MASKED)
        probs = jnp.exp(scores - log_ref[h : h + 1, :])
        probs_back = dot(value, grad, 1, 1)
        score_back = (probs * (probs_back - dots[h : h + 1, :])).astype(BF)
        value_back = jnp.where(lane == h, dot(probs.astype(BF), grad, 1, 0), value_back)
        key_back = jnp.where(lane == h, dot(score_back, query, 1, 0), key_back)
        sums[...] += dot(score_back, key, 0, 0)
    out[pl.ds(start, block), LANES : 2 * LANES] = key_back.astype(BF)
    out[pl.ds(start, block), 2 * LANES :] = value_back.astype(BF)

    @pl.when(step == pl.num_programs(0) - 1)
    def _():
        out[:, :LANES] = (sums[...] * HD**-0.5).astype(BF)


def attention_backward(pair, projected, table, grads, attended, logs):
    length = projected.shape[0]
    block = min(512, length)

    def column(c):
        return pl.BlockSpec((length, LANES), lambda i, t: (0, c))

    return pl.pallas_call(
        partial(backward_kernel, block=block, count=table.shape[0] - 2),
        grid_spec=pltpu.PrefetchScalarGridSpec(
            num_scalar_prefetch=1,
            grid=(length // block,),
            in_specs=[
                column(3 * pair),
                pl.BlockSpec((block, LANES), lambda i, t: (i, 3 * pair + 1)),
                pl.BlockSpec((block, LANES), lambda i, t: (i, 3 * pair + 2)),
                fixed((8, length), pair, 0),
            ]
            + [fixed((value.shape[0], LANES), 0, pair) for value in (*grads, *attended)],
            out_specs=fixed((length, 3 * LANES)),
            scratch_shapes=[
                pltpu.VMEM((length, LANES), F32),
                pltpu.VMEM((8, length), F32),
                pltpu.VMEM((length, LANES), BF),
            ],
        ),
        out_shape=jax.ShapeDtypeStruct((length, 3 * LANES), BF),
        cost_estimate=about(30, 4.0),
        compiler_params=pltpu.CompilerParams(vmem_limit_bytes=56 << 20),
        name="attention_backward",
    )(table, projected, projected, projected, logs, *grads, *attended)


def adamw_kernel(scale_ref, *refs, turned, parts):
    clip, fix_one, fix_two = scale_ref[0], scale_ref[1], scale_ref[2]
    step = pl.program_id(0)
    grads, ins, outs = refs[: 6 + parts], refs[6 + parts : 27 + parts], refs[27 + parts :]

    def update(k, grad):
        param, moment, square = (ref[...] for ref in ins[3 * k : 3 * k + 3])
        grad_ref, moment_ref, square_ref, change_ref = outs[4 * k : 4 * k + 4]
        clipped = grad * clip
        moment_new = BETA_ONE * moment + (1.0 - BETA_ONE) * clipped
        square_new = BETA_TWO * square + (1.0 - BETA_TWO) * clipped * clipped
        grad_ref[...] = grad
        moment_ref[...] = moment_new
        square_ref[...] = square_new
        change_ref[...] = -RATE * (
            moment_new / fix_one / (jnp.sqrt(square_new / fix_two) + ADAM_EPS) + DECAY * param
        )

    update(
        0,
        jnp.stack(
            [
                jnp.concatenate([ref[:, c * LANES : (c + 1) * LANES] for ref in grads[:parts]], axis=1)
                for c in range(3)
            ]
        ),
    )
    update(2, grads[parts + 1][...].astype(F32))
    update(3, jnp.transpose(grads[parts + 2][...].astype(F32)))

    @pl.when(step < turned)
    def _():
        update(1, jnp.transpose(grads[parts][...]))

    @pl.when(step == 0)
    def _():
        for k in range(3):
            update(4 + k, grads[parts + 3 + k][...])


def in_hbm(value):
    return pltpu.with_memory_space_constraint(value, pltpu.HBM)


def adamw(scales, attend_parts, others, params, firsts, squares):
    shard = params[0].shape[1]
    steps = params[3].shape[0] // LANES
    turned = params[1].shape[0] // LANES
    rows = shard // steps

    def last(i):
        return jnp.minimum(i, turned - 1)

    state = [
        pl.BlockSpec((3, rows, params[0].shape[2]), lambda i: (0, i, 0)),
        pl.BlockSpec((LANES, shard), lambda i: (last(i), 0)),
        pl.BlockSpec((rows, params[2].shape[1]), lambda i: (i, 0)),
        pl.BlockSpec((LANES, shard), lambda i: (i, 0)),
    ] + [pl.BlockSpec(value.shape, lambda i: (0, 0)) for value in params[4:]]
    grad_specs = (
        [pl.BlockSpec((rows, 3 * LANES), lambda i: (i, 0)) for _ in attend_parts]
        + [
            pl.BlockSpec((shard, LANES), lambda i: (0, last(i))),
            state[2],
            pl.BlockSpec((shard, LANES), lambda i: (0, i)),
        ]
        + state[4:]
    )
    ins = [in_hbm(value) for group in zip(params, firsts, squares) for value in group]
    return pl.pallas_call(
        partial(adamw_kernel, turned=turned, parts=len(attend_parts)),
        grid=(steps,),
        in_specs=[smem()] + grad_specs + [spec for spec in state for _ in range(3)],
        out_specs=[spec for spec in state for _ in range(4)],
        out_shape=[jax.ShapeDtypeStruct(value.shape, F32) for value in params for _ in range(4)],
        cost_estimate=about(6),
        compiler_params=pltpu.CompilerParams(vmem_limit_bytes=50 << 20),
        name="adamw",
    )(scales, *attend_parts, *others, *ins)


def local(
    tokens,
    cotangent,
    lengths,
    attend,
    mixing,
    expand,
    contract,
    outer_norms,
    head_norms,
    unit_norms,
    attend_moment,
    mixing_moment,
    expand_moment,
    contract_moment,
    outer_moment,
    head_moment,
    unit_moment,
    attend_square,
    mixing_square,
    expand_square,
    contract_square,
    outer_square,
    head_square,
    unit_square,
):
    height = tokens.shape[0]
    shard_count = lax.axis_size("mp")
    device_count = lax.axis_size("dp") * shard_count
    length_all = height * shard_count
    place = lax.axis_index("mp")
    sequences = lengths.shape[1]
    head_width = attend.shape[2]
    unit_width = expand.shape[1]
    shard = attend.shape[1]
    pairs = head_width // LANES
    step = height
    everything = Rows(list(range(shard_count)), height, step)
    near = Rows([0, 1], height, step)
    far = Rows(list(range(2, shard_count)), height, step)
    table = jnp.concatenate([lengths[0], jnp.stack([place * height, place]).astype(jnp.int32)])

    by_pair = attend.astype(BF).reshape(3, shard, pairs, LANES).transpose(1, 2, 0, 3)
    by_pair = by_pair.reshape(shard, 3 * head_width)
    work_even = gather_groups(jnp.concatenate([by_pair, mixing.astype(BF).T], axis=1))

    sizes = [x.size for x in (outer_norms, head_norms, unit_norms)]
    starts = [0, sizes[0], sizes[0] + sizes[1]]
    packed = jnp.concatenate([outer_norms.reshape(-1), head_norms.reshape(-1), unit_norms.reshape(-1)])
    tables = exchange_all(jnp.broadcast_to(packed[None], (device_count, packed.shape[0])))

    token_near, token_even = gather_near(tokens)
    work_odd = cross_groups(work_even, [*token_even, tables])
    token_far = gather_far(after(token_even, work_odd))
    work_in, work_mix = place_groups(work_even, work_odd, [3 * head_width, head_width])
    wide_shard = after(
        [jnp.concatenate([expand.astype(BF), contract.astype(BF).T], axis=1)], [work_in]
    )[0]
    weights = lax.all_gather(wide_shard, "dp", axis=0, tiled=True)

    def unpack(k, rows):
        part = tables[:, starts[k] : starts[k] + sizes[k]].reshape(device_count, rows, -1)
        return part.transpose(1, 0, 2).reshape(rows, -1)

    outer = unpack(0, 4)
    head_gains = unpack(1, 2)
    unit_local = lax.dynamic_slice_in_dim(unpack(2, 2), place * unit_width, unit_width, 1)
    normed_all, projected = project(everything, token_near + token_far, work_in, outer)
    mix_near, mix_even = gather_near(work_mix)
    attended, logs = attention_forward(everything, projected, table)
    back_near, back_even = gather_near(after([cotangent], [normed_all])[0])
    attended, logs, mix_near, mix_even, back_even = lax.optimization_barrier(
        (attended, logs, mix_near, mix_even, back_even)
    )
    mixes = mix_near + gather_far(mix_even)
    head_blocks = [attended[0]] + [swap(attended[r], r) for r in range(1, shard_count)]
    middle, mid_own, mixed_in = mix_rows(
        table, sequences, head_blocks, mixes, head_gains, tokens, outer
    )
    mid_near, mid_even = gather_near(mid_own)
    cotangent_blocks = back_near + gather_far(back_even)

    back_all, unit_in = feed_back(everything, cotangent_blocks, table, sequences, weights)
    kept = widen(near, mid_near, weights, unit_in, unit_local)
    mid_far = gather_far(after(mid_even, kept))
    mid_all, activated, slopes, sums = widen(far, mid_far, weights, unit_in, unit_local, kept)
    unit_totals = token_totals(sums)
    low_far, wide_far, sums_far, *far_terms = narrow_back(
        far, activated, slopes, unit_in, unit_totals, unit_local, weights
    )
    far_sums = [value.astype(BF) for value in sum_chip(far_terms)]
    arrived = sum_far(far_sums)
    late_slopes = after([slopes], far_sums)[0]
    unit_low, widened_low, sums_near, *near_terms = narrow_back(
        near, activated, late_slopes, unit_in, unit_totals, unit_local, weights, (low_far, wide_far)
    )
    contract_back = weight_grad(back_all, unit_low)
    arrived = after(arrived, [*near_terms, contract_back])
    mid_terms = [near_terms[0], swap(near_terms[1], 1), *arrived]
    middle_back, middle_low, outer_sums, head_sums, *head_grads = mix_rows_back(
        table, sequences, mid_terms, middle, cotangent, outer, head_blocks, mixes, head_gains
    )

    grad_even = [head_grads[0]] + [swap(head_grads[r], r) for r in range(1, shard_count)]
    feed_terms = feed_rows(everything, after([unit_low], [middle_low])[0], weights)
    expand_back = weight_grad(mid_all, after([widened_low], [middle_low])[0])
    mix_terms = mix_grads(middle_low, mixed_in, shard_count)
    grad_blocks = [grad_even[0]] + after(grad_even[1:], [*feed_terms, *mix_terms, expand_back])

    def column_sums(value):
        return jnp.sum(value.reshape(2, 8, -1), axis=1)

    def for_owners(value):
        return value.reshape(value.shape[0], device_count, -1).transpose(1, 0, 2).reshape(device_count, -1)

    unit_sums = lax.dynamic_update_slice_in_dim(
        jnp.zeros((2, FF), F32), column_sums(sums_near + sums_far), place * unit_width, 1
    )
    terms = jnp.concatenate(
        [
            for_owners(column_sums(outer_sums)),
            for_owners(column_sums(head_sums)),
            for_owners(unit_sums),
        ],
        axis=1,
    )
    feed_sums = [value.astype(BF) for value in sum_chip(feed_terms[2:])]
    mix_sums = [value.astype(BF) for value in sum_chip(mix_terms[2:])]
    grad_blocks = after(grad_blocks, [*feed_sums, *mix_sums])
    term_sums = exchange_all(after([terms], grad_blocks)[0])
    *mix_sums, last = after([*mix_sums, feed_sums[-1]], grad_blocks)
    mix_arrived = sum_far(mix_sums)
    feed_arrived = sum_far([*feed_sums[:-1], last])
    backs = [attention_backward(0, projected, table, grad_blocks, attended, logs)]
    backs, feed_arrived, mix_arrived, term_sums = lax.optimization_barrier(
        (backs, feed_arrived, mix_arrived, term_sums)
    )
    mix_terms = [mix_terms[0], swap(mix_terms[1], 1), *mix_arrived]
    pieces = [exchange_groups(attend_rows(normed_all, backs[0], mix_terms))]
    for pair in range(1, pairs):
        backs.append(attention_backward(pair, projected, table, grad_blocks, attended, logs))
        value = after([attend_rows(normed_all, backs[-1])], pieces)[0]
        pieces.append(exchange_groups(value))
        late = after(backs, [value])

    def scatter(value):
        return lax.psum_scatter(value, "dp", scatter_dimension=0, tiled=True)

    contract_grad = scatter(contract_back)
    expand_grad = scatter(expand_back)
    if pairs == 1:
        late = backs
    far_terms = input_back(far, late, work_in)
    far_sums = [value.astype(BF) for value in sum_chip(far_terms)]
    near_terms = input_back(near, after(late, far_sums), work_in)
    arrived = sum_far(far_sums)
    outer, expand_late, contract_late, term_sums = after(
        [outer, expand_grad, contract_grad, term_sums], near_terms
    )

    local_squares = jnp.float32(0.0)
    for gradient in [expand_late, contract_late]:
        local_squares = local_squares + jnp.sum(jnp.square(gradient.astype(F32)))
    local_squares, near_terms, pieces = lax.optimization_barrier((local_squares, near_terms, pieces))
    norm_sums = jnp.sum(term_sums, axis=0)
    outer_rows = lax.dynamic_slice_in_dim(outer, lax.axis_index("dp") * shard, shard, 1).T
    attend_parts, outer_terms = [], 0.0
    for pair, piece in enumerate(pieces):
        grad, sums, *beside = attend_sums(
            piece, by_pair[:, 3 * LANES * pair : 3 * LANES * (pair + 1)], outer_rows, 3 * LANES
        )
        attend_parts.append(grad)
        outer_terms = outer_terms + sums
        if beside:
            mixing_grad = beside[0]
    outer_terms = outer_terms.T
    for bit in mp_bits():
        outer_terms = outer_terms + swap(outer_terms, bit)
    own_norms = outer_norms.shape[1]
    first_grad = lax.dynamic_slice_in_dim(outer_terms, place * own_norms, own_norms, 1)
    half = sizes[0] // 2
    norm_grads = [
        jnp.concatenate([first_grad, norm_sums[:half].reshape(2, own_norms)], axis=0),
        norm_sums[half : half + sizes[1]].reshape(head_norms.shape),
        norm_sums[half + sizes[1] :].reshape(unit_norms.shape),
    ]

    for gradient in [*norm_grads, mixing_grad, *attend_parts]:
        local_squares = local_squares + jnp.sum(gradient * gradient)
    all_squares = exchange_all(jnp.broadcast_to(local_squares, (device_count, 128)))
    result = middle + sum_near(feed_terms[:2], after(feed_arrived, [local_squares]))
    result = result.astype(BF)
    normed_back = sum_near(near_terms, arrived)
    inputs = tokens.astype(F32)
    first_normed, first_factor = norm_rows(inputs)
    input_grad = middle_back + norm_back(normed_back, first_normed, first_factor, outer[0])[0]
    all_squares, input_grad, result = lax.optimization_barrier((all_squares, input_grad, result))
    norm = jnp.sqrt(jnp.sum(all_squares[:, 0]))
    clip = jnp.minimum(1.0, MAX_NORM / (norm + 1e-06))
    count_steps = jnp.float32(ADAM_STEP)
    fix_one = 1.0 - jnp.power(jnp.float32(BETA_ONE), count_steps)
    fix_two = 1.0 - jnp.power(jnp.float32(BETA_TWO), count_steps)
    results = adamw(
        jnp.stack([clip, fix_one, fix_two]),
        attend_parts,
        [mixing_grad, expand_grad, contract_grad, *norm_grads],
        (attend, mixing, expand, contract, outer_norms, head_norms, unit_norms),
        (
            attend_moment,
            mixing_moment,
            expand_moment,
            contract_moment,
            outer_moment,
            head_moment,
            unit_moment,
        ),
        (
            attend_square,
            mixing_square,
            expand_square,
            contract_square,
            outer_square,
            head_square,
            unit_square,
        ),
    )
    return (result, input_grad, norm, *results)


def solution(mesh):
    rows = P(ALL, None)
    norms = P(None, ALL)
    weights = (P(None, "dp", "mp"), P("mp", "dp"), P("dp", "mp"), P("mp", "dp"))
    states = weights + (norms,) * 3
    outs = (rows, rows, P())
    for spec in states:
        outs = outs + (spec,) * 4
    return jax.shard_map(
        local,
        mesh=mesh,
        in_specs=(rows, rows, P("dp", None)) + states * 3,
        out_specs=outs,
        check_vma=False,
    )
```

```python
from functools import partial

import jax
import jax.numpy as jnp
from jax import lax
from jax.experimental import pallas as pl
from jax.experimental.pallas import tpu as pltpu
from jax.sharding import PartitionSpec as P

D = 1024
HD = 64
FF = 4096
ADAM_STEP = 10

NORM_EPS = 1e-05
MASKED = -1e30
RATE = 0.02
BETA_ONE = 0.9
BETA_TWO = 0.95
ADAM_EPS = 1e-08
DECAY = 0.1
MAX_NORM = 1.0

BF = jnp.bfloat16
F32 = jnp.float32
ALL = ("dp", "mp")


def swap(value, bit):
    count = lax.axis_size("mp")
    return lax.ppermute(value, "mp", [(i, i ^ bit) for i in range(count)])


def mp_bits():
    count = lax.axis_size("mp")
    return [1 << b for b in range(count.bit_length() - 1)]


def after(values, others):
    values, _ = lax.optimization_barrier((tuple(values), tuple(others)))
    return list(values)


def gather_near(own):
    even = {0: own}
    for bit in reversed(mp_bits()[1:]):
        for r in list(even):
            even[r | bit] = swap(even[r], bit)
    return [own, swap(own, 1)], [even[r] for r in range(2, 2 * len(even), 2)]


def gather_far(even):
    return [block for value in even for block in (value, swap(value, 1))]


def sum_chip(terms):
    return [
        terms[2 * i].astype(F32) + swap(terms[2 * i + 1], 1).astype(F32)
        for i in range(len(terms) // 2)
    ]


def sum_far(sums):
    even = {2 * i + 2: value for i, value in enumerate(sums)}
    arrived = []
    for bit in mp_bits()[1:]:
        for r in [r for r in even if r & bit]:
            received = swap(even.pop(r).astype(BF), bit)
            if r == bit:
                arrived.append(received)
            else:
                even[r ^ bit] = even[r ^ bit].astype(F32) + received.astype(F32)
    return arrived


def sum_near(terms, arrived):
    total = terms[0].astype(F32) + swap(terms[1], 1).astype(F32)
    for value in arrived:
        total = total + value.astype(F32)
    return total


def token_totals(values):
    count = lax.axis_size("mp")
    height = values.shape[1] // count
    for bit in mp_bits():
        received = swap(values, bit)
        parts = [received[:, (r ^ bit) * height : ((r ^ bit) + 1) * height] for r in range(count)]
        values = values + jnp.concatenate(parts, axis=1)
    return values


def exchange_all(value):
    return lax.all_to_all(value, ALL, 0, 0, tiled=True)


def dp_swap(value, bits):
    count = lax.axis_size("dp")
    return lax.ppermute(value, "dp", [(i, i ^ bits) for i in range(count)])


def place_kernel(table_ref, *refs):
    blocks, outs = refs[:8], refs[8:]
    rows = blocks[0].shape[0]
    for r, ref in enumerate(blocks):
        start = pl.multiple_of((table_ref[0] ^ r) * rows, rows)
        first = 0
        for out in outs:
            out[pl.ds(start, rows), :] = ref[:, first : first + out.shape[1]]
            first += out.shape[1]


def smem():
    return pl.BlockSpec(memory_space=pltpu.SMEM)


def vmem():
    return pl.BlockSpec(memory_space=pltpu.VMEM)


def gather_groups(shard):
    if lax.axis_size("dp") != 8:
        return [lax.all_gather(shard, "dp", axis=0, tiled=True)]
    return [shard] + [dp_swap(shard, bits) for bits in (2, 4, 6)]


def cross_groups(even, others):
    if len(even) == 1:
        return []
    first = dp_swap(even[0], 1)
    odd = [first, dp_swap(first, 2)]
    return odd + [dp_swap(value, 1) for value in after(even[2:], odd + even[1:2] + others)]


def place_groups(even, odd, widths):
    if len(even) == 1:
        return list(jnp.split(even[0], [sum(widths[: k + 1]) for k in range(len(widths) - 1)], axis=1))
    blocks = [block for both in zip(even, odd) for block in both]
    place = lax.axis_index("dp").astype(jnp.int32)[None]
    rows = even[0].shape[0]
    return pl.pallas_call(
        place_kernel,
        in_specs=[smem()] + [vmem()] * 8,
        out_specs=[vmem()] * len(widths),
        out_shape=[jax.ShapeDtypeStruct((8 * rows, width), even[0].dtype) for width in widths],
        cost_estimate=about(2),
        name="place_rows",
    )(place, *blocks)


def exchange_groups(value):
    return lax.all_to_all(value, "dp", 0, 0, tiled=True)


HINT = 4.0


def about(microseconds, hint=HINT):
    return pl.CostEstimate(
        flops=int(microseconds * hint * 1.15e9),
        transcendentals=0,
        bytes_accessed=int(microseconds * hint * 1e5),
    )


def dot(left, right, left_dim, right_dim):
    return lax.dot_general(
        left, right, (((left_dim,), (right_dim,)), ((), ())), preferred_element_type=F32
    )


def norm_rows(value):
    mean = jnp.mean(value, axis=-1, keepdims=True)
    centered = value - mean
    variance = jnp.mean(centered * centered, axis=-1, keepdims=True)
    factor = lax.rsqrt(variance + NORM_EPS)
    return centered * factor, factor


def norm_back(grad, normed, factor, gain):
    weighted = grad * gain
    result = factor * (
        weighted
        - jnp.mean(weighted, axis=-1, keepdims=True)
        - normed * jnp.mean(weighted * normed, axis=-1, keepdims=True)
    )
    return result, jnp.sum(grad * normed, axis=0), jnp.sum(grad, axis=0)


def as_rows(columns, count):
    rows = columns[0].shape[0]
    lane = lax.broadcasted_iota(jnp.int32, (rows, 128), 1)
    spread = jnp.zeros((rows, 128), F32)
    for i, column in enumerate(columns):
        spread = jnp.where(lane == i, column, spread)
    return jnp.transpose(spread)[:count]


def as_columns(values):
    count, rows = values.shape
    padded = jnp.concatenate([values, jnp.zeros((128 - count, rows), F32)], axis=0)
    turned = jnp.transpose(padded)
    return [turned[:, i : i + 1] for i in range(count)]


def fold(value):
    return jnp.sum(value.reshape(value.shape[0] // 8, 8, value.shape[1]), axis=0)


def moments(first, second, width):
    mean = first / width
    variance = second / width - mean * mean
    return mean, lax.rsqrt(variance + NORM_EPS)


class Rows:
    def __init__(self, blocks, height, step):
        self.blocks = blocks
        self.per = height // step
        self.step = step
        self.height = height
        self.grid = (len(blocks) * self.per,)

    def at(self, i):
        return i + self.blocks[0] * self.per

    def whole(self, width, column=0):
        return pl.BlockSpec((self.step, width), lambda i, *t: (self.at(i), column))

    def stats(self, count):
        return pl.BlockSpec((count, self.step), lambda i, *t: (0, self.at(i)))

    def pieces(self, width):
        per = self.per
        return [
            pl.BlockSpec(
                (self.step, width), lambda i, *t, first=k * per: (jnp.clip(i - first, 0, per - 1), 0)
            )
            for k in range(len(self.blocks))
        ]

    def load(self, refs, into):
        for k, ref in enumerate(refs):

            @pl.when(pl.program_id(0) // self.per == k)
            def _():
                into[...] = ref[...]

    def store(self, refs, value):
        for k, ref in enumerate(refs):

            @pl.when(pl.program_id(0) // self.per == k)
            def _():
                ref[...] = value


def fixed(shape, *index):
    index = index or (0,) * len(shape)
    return pl.BlockSpec(shape, lambda i, *t: index)


ANY = pl.BlockSpec(memory_space=pl.ANY)


def call(kernel, part, name, ins, in_specs, outs, out_specs, scratch=(), kept=None, table=None, cost=8, pieces=False):
    ins, in_specs = list(ins), list(in_specs)
    aliases = {}
    tables = [] if table is None else [table]
    if kept is not None:
        for k, value in enumerate(kept):
            aliases[len(tables) + len(ins)] = k
            ins.append(value)
            in_specs.append(ANY)
    dropped = 0 if kept is None else len(kept)
    used = len(tables) + len(ins) - dropped

    def body(*refs):
        kernel(*refs[:used], *refs[used + dropped :])

    hbm = len(outs) - len(part.blocks) if pieces else len(outs)
    return pl.pallas_call(
        body,
        grid_spec=pltpu.PrefetchScalarGridSpec(
            num_scalar_prefetch=len(tables),
            grid=part.grid,
            in_specs=in_specs,
            out_specs=list(out_specs),
            scratch_shapes=list(scratch),
        ),
        out_shape=[jax.ShapeDtypeStruct(*out) for out in outs[:hbm]]
        + [pltpu.HBM(*out) for out in outs[hbm:]],
        input_output_aliases=aliases,
        cost_estimate=about(cost * len(part.blocks) / 4),
        compiler_params=pltpu.CompilerParams(vmem_limit_bytes=50 << 20),
        name=name,
    )(*tables, *ins)


def project(part, blocks, work_in, outer):
    count, length = len(blocks), len(blocks) * part.height
    width = work_in.shape[1]

    def kernel(*refs):
        work_ref, gain_ref, normed_ref, out_ref, row = refs[count:]
        part.load(refs[:count], row)
        normed = norm_rows(row[...].astype(F32))[0]
        normed_ref[...] = normed.astype(BF)
        normed = (normed * gain_ref[0:1] + gain_ref[1:2]).astype(BF)
        out_ref[...] = dot(normed, work_ref[...], 1, 0).astype(BF)

    return call(
        kernel,
        part,
        "project",
        [*blocks, work_in, outer],
        [*part.pieces(D), fixed(work_in.shape), fixed(outer.shape)],
        [((length, D), BF), ((length, width), BF)],
        [part.whole(D), part.whole(width)],
        [pltpu.VMEM((part.step, D), BF)],
    )


def columns_of(table_ref, index, r, width):
    return pl.ds(pl.multiple_of((table_ref[index] ^ r) * width, width), width)


def head_norm(att_refs):
    parts = [ref[...].astype(F32) for ref in att_refs]
    mean = sum(jnp.sum(part, axis=1, keepdims=True) for part in parts) / D
    parts = [part - mean for part in parts]
    variance = sum(jnp.sum(part * part, axis=1, keepdims=True) for part in parts) / D
    factor = lax.rsqrt(variance + NORM_EPS)
    return [part * factor for part in parts], factor


def own_call(kernel, name, table, ins, in_specs, outs, out_specs, height, cost, scratch=()):
    return pl.pallas_call(
        kernel,
        grid_spec=pltpu.PrefetchScalarGridSpec(
            num_scalar_prefetch=1,
            grid=(height // OWN_STEP,),
            in_specs=in_specs,
            out_specs=out_specs,
            scratch_shapes=list(scratch),
        ),
        out_shape=[pltpu.HBM(*out) if out[1] == BF else jax.ShapeDtypeStruct(*out) for out in outs],
        cost_estimate=about(cost),
        compiler_params=pltpu.CompilerParams(vmem_limit_bytes=50 << 20),
        name=name,
    )(table, *ins)


OWN_STEP = 256


def own(width):
    return pl.BlockSpec((OWN_STEP, width), lambda i, t: (i, 0))


def mix_rows(table, sequences, blocks, mixes, gains, tokens, outer):
    count, (height, width) = len(blocks), blocks[0].shape

    def kernel(table_ref, *refs):
        att_refs, mix_refs = refs[:count], refs[count : 2 * count]
        gain_ref, token_ref, outer_ref, middle_ref, mid_ref, in_ref = refs[2 * count :]
        middle = token_ref[...].astype(F32)
        for r, normed in enumerate(head_norm(att_refs)[0]):
            columns = columns_of(table_ref, sequences + 1, r, width)
            low = (normed * gain_ref[0:1, columns] + gain_ref[1:2, columns]).astype(BF)
            in_ref[:, r * width : (r + 1) * width] = low
            middle = middle + dot(low, mix_refs[r][...], 1, 1)
        middle_ref[...] = middle
        mid_ref[...] = (norm_rows(middle)[0] * outer_ref[2:3] + outer_ref[3:4]).astype(BF)

    return own_call(
        kernel,
        "mix_rows",
        table,
        [*blocks, *mixes, gains, tokens, outer],
        [own(width)] * count + [fixed((D, width))] * count + [fixed((2, D)), own(D), fixed((4, D))],
        [((height, D), F32), ((height, D), BF), ((height, D), BF)],
        [own(D)] * 3,
        height,
        6,
    )


def mix_rows_back(table, sequences, terms, middle, cotangent, outer, blocks, mixes, gains):
    count, (height, width) = len(blocks), blocks[0].shape

    def kernel(table_ref, *refs):
        term_refs, refs = refs[: len(terms)], refs[len(terms) :]
        middle_ref, back_ref, outer_ref, gain_ref = refs[:4]
        att_refs, mix_refs = refs[4 : 4 + count], refs[4 + count : 4 + 2 * count]
        out_ref, low_ref, outer_sum, head_sum, *outs = refs[4 + 2 * count :]

        @pl.when(pl.program_id(0) == 0)
        def _():
            outer_sum[...] = jnp.zeros_like(outer_sum)
            head_sum[...] = jnp.zeros_like(head_sum)

        grad = sum(ref[...].astype(F32) for ref in term_refs)
        normed, factor = norm_rows(middle_ref[...])
        weighted = grad * outer_ref[2:3]
        first = jnp.mean(weighted, axis=1, keepdims=True)
        second = jnp.mean(weighted * normed, axis=1, keepdims=True)
        outer_sum[0:8] += fold(grad * normed)
        outer_sum[8:16] += fold(grad)
        rows = pl.program_id(0) * OWN_STEP + lax.broadcasted_iota(jnp.int32, (OWN_STEP, 1), 0)
        live = segments_at(rows, table_ref, sequences) < sequences
        back = jnp.where(live, back_ref[...].astype(F32), 0.0)
        back = back + factor * (weighted - first - normed * second)
        out_ref[...] = back
        low = back.astype(BF)
        low_ref[...] = low
        normed, factor = head_norm(att_refs)
        weighted = []
        first, second = 0.0, 0.0
        for r in range(count):
            columns = columns_of(table_ref, sequences + 1, r, width)
            grad = dot(low, mix_refs[r][...], 1, 0)
            head_sum[0:8, columns] += fold(grad * normed[r])
            head_sum[8:16, columns] += fold(grad)
            weighted.append(grad * gain_ref[0:1, columns])
            first = first + jnp.sum(weighted[r], axis=1, keepdims=True)
            second = second + jnp.sum(weighted[r] * normed[r], axis=1, keepdims=True)
        for r in range(count):
            value = factor * (weighted[r] - first / D - normed[r] * (second / D))
            outs[r][...] = value.astype(BF)

    return own_call(
        kernel,
        "mix_rows_back",
        table,
        [*terms, middle, cotangent, outer, gains, *blocks, *mixes],
        [own(D)] * (len(terms) + 2)
        + [fixed((4, D)), fixed((2, D))]
        + [own(width)] * count
        + [fixed((D, width))] * count,
        [((height, D), F32), ((height, D), BF), ((16, D), F32), ((16, D), F32)]
        + [((height, width), BF)] * count,
        [own(D), own(D), fixed((16, D)), fixed((16, D))] + [own(width)] * count,
        height,
        8,
    )


def mix_grads(low, mixed_in, count):
    height, width = low.shape[0], mixed_in.shape[1] // count
    block = 256

    def kernel(low_ref, in_ref, *outs):
        for r in range(count):
            outs[r][...] = dot(low_ref[...], in_ref[:, r * width : (r + 1) * width], 0, 0).astype(BF)

    return pl.pallas_call(
        kernel,
        grid=(D // block,),
        in_specs=[
            pl.BlockSpec((height, block), lambda i: (0, i)),
            pl.BlockSpec((height, D), lambda i: (0, 0)),
        ],
        out_specs=[pl.BlockSpec((block, width), lambda i: (i, 0))] * count,
        out_shape=[pltpu.HBM((D, width), BF)] * count,
        cost_estimate=about(4),
        compiler_params=pltpu.CompilerParams(vmem_limit_bytes=50 << 20),
        name="mix_grads",
    )(low, mixed_in)


def feed_back(part, blocks, table, sequences, weights):
    count, length = len(blocks), len(blocks) * part.height
    units = weights.shape[1] // 2

    def kernel(table_ref, *refs):
        work_ref, back_ref, out_ref, row = refs[count:]
        part.load(refs[:count], row)
        rows = pl.program_id(0) * part.step + lax.broadcasted_iota(jnp.int32, (part.step, 1), 0)
        live = segments_at(rows, table_ref, sequences) < sequences
        back = jnp.where(live, row[...].astype(F32), 0.0).astype(BF)
        back_ref[...] = back
        out_ref[...] = dot(back, work_ref[...], 1, 0).astype(BF)

    return call(
        kernel,
        part,
        "feed_back",
        [*blocks, weights],
        [*part.pieces(D), fixed((D, units), 0, 1)],
        [((length, D), BF), ((length, units), BF)],
        [part.whole(D), part.whole(units)],
        [pltpu.VMEM((part.step, D), BF)],
        table=table,
    )


def widen(part, blocks, weights, unit_in, gains, kept=None):
    count, (length, units) = len(blocks), unit_in.shape

    def kernel(*refs):
        work_ref, in_ref, gain_ref, mid_ref, act_ref, slope_ref, total_ref, row = refs[count:]
        part.load(refs[:count], row)
        mid_ref[...] = row[...]
        wide = dot(row[...], work_ref[...], 1, 0)
        share = 0.5 + 0.5 * lax.erf(wide * 0.7071067811865476)
        act = wide * share
        act_ref[...] = act
        slope_ref[...] = (share + wide * (0.3989422804014327 * jnp.exp(-0.5 * wide * wide))).astype(BF)
        weighted = in_ref[...].astype(F32) * gain_ref[0:1]
        values = (act, act * act, weighted, weighted * act)
        total_ref[...] = as_rows([jnp.sum(v, axis=1, keepdims=True) for v in values], 4)

    return call(
        kernel,
        part,
        "widen",
        [*blocks, weights, unit_in, gains],
        [*part.pieces(D), fixed((D, units), 0, 0), part.whole(units), fixed(gains.shape)],
        [((length, D), BF), ((length, units), F32), ((length, units), BF), ((4, length), F32)],
        [part.whole(D), part.whole(units), part.whole(units), part.stats(4)],
        [pltpu.VMEM((part.step, D), BF)],
        kept=kept,
    )


NARROW_ROWS = 64
NARROW_COLUMNS = 256


def narrow_back(part, act, slope, unit_in, totals, gains, weights, kept=None):
    length, units = act.shape

    def kernel(act_ref, slope_ref, in_ref, total_ref, gain_ref, work_ref, low_ref, wide_ref, sum_ref, *outs):
        first, second, third, fourth = as_columns(total_ref[...])
        mean, factor = moments(first, second, FF)
        inner = factor * (fourth - mean * third)

        @pl.when(pl.program_id(0) == 0)
        def _():
            sum_ref[...] = jnp.zeros_like(sum_ref)

        for start in range(0, part.step, NARROW_ROWS):
            rows = slice(start, start + NARROW_ROWS)
            for left in range(0, units, NARROW_COLUMNS):
                columns = slice(left, left + NARROW_COLUMNS)
                gain, bias = gain_ref[0:1, columns], gain_ref[1:2, columns]
                normed = (act_ref[rows, columns] - mean[rows]) * factor[rows]
                low_ref[rows, columns] = (normed * gain + bias).astype(BF)
                grad = in_ref[rows, columns].astype(F32)
                back = factor[rows] * (grad * gain - third[rows] / FF - normed * (inner[rows] / FF))
                wide_ref[rows, columns] = (back * slope_ref[rows, columns].astype(F32)).astype(BF)
                sum_ref[0:8, columns] += fold(grad * normed)
                sum_ref[8:16, columns] += fold(grad)
        part.store(outs, dot(wide_ref[...], work_ref[...], 1, 1).astype(BF))

    return call(
        kernel,
        part,
        "narrow_back",
        [act, slope, unit_in, totals, gains, weights],
        [part.whole(units)] * 3 + [part.stats(4), fixed(gains.shape), fixed((D, units), 0, 0)],
        [((length, units), BF)] * 2
        + [((16, units), F32)]
        + [((part.height, D), BF)] * len(part.blocks),
        [part.whole(units)] * 2 + [fixed((16, units))] + part.pieces(D),
        kept=kept,
        pieces=True,
    )


def weight_grad(left, right):
    length, block = left.shape[0], 256

    def kernel(left_ref, right_ref, out_ref):
        out_ref[...] = dot(left_ref[...], right_ref[...], 0, 0).astype(BF)

    return pl.pallas_call(
        kernel,
        grid=(left.shape[1] // block,),
        in_specs=[
            pl.BlockSpec((length, block), lambda i: (0, i)),
            pl.BlockSpec(right.shape, lambda i: (0, 0)),
        ],
        out_specs=pl.BlockSpec((block, right.shape[1]), lambda i: (i, 0)),
        out_shape=jax.ShapeDtypeStruct((left.shape[1], right.shape[1]), BF),
        cost_estimate=about(8),
        compiler_params=pltpu.CompilerParams(vmem_limit_bytes=50 << 20),
        name="weight_grad",
    )(left, right)


def feed_rows(part, low, weights):
    units = low.shape[1]

    def kernel(low_ref, work_ref, *outs):
        part.store(outs, dot(low_ref[...], work_ref[...], 1, 1).astype(BF))

    return call(
        kernel,
        part,
        "feed_rows",
        [low, weights],
        [part.whole(units), fixed((D, units), 0, 1)],
        [((part.height, D), BF)] * len(part.blocks),
        part.pieces(D),
        pieces=True,
    )


EXTRA = 16


def attend_rows(normed_all, back, extra=()):
    length, width = back.shape
    groups = lax.axis_size("dp")
    shard = D // groups
    more = extra[0].shape[1] if extra else 0

    def kernel(normed_ref, back_ref, *refs):
        out_ref, total_ref = refs[-2:]

        @pl.when(pl.program_id(0) == 0)
        def _():
            value = jnp.sum(fold(back_ref[...].astype(F32)), axis=0, keepdims=True)
            row = lax.broadcasted_iota(jnp.int32, (EXTRA, width), 0)
            total = jnp.zeros((EXTRA, width), F32)
            for k in range(3):
                piece = value.astype(BF).astype(F32)
                total = jnp.where(row == k, piece, total)
                value = value - piece
            total_ref[...] = total.astype(BF)

        start = pl.multiple_of(pl.program_id(0) * shard, shard)
        if shard % 128 == 0:
            normed = normed_ref[:, pl.ds(start, shard)]
        else:
            normed = normed_ref[...]
        out_ref[0, :shard, :width] = dot(normed, back_ref[...], 0, 0).astype(BF)
        out_ref[0, shard:, :width] = total_ref[...]
        if extra:
            value = sum(ref[...].astype(F32) for ref in refs[:-2])
            out_ref[0, :shard, width:] = value.astype(BF)
            out_ref[0, shard:, width:] = jnp.zeros((EXTRA, more), BF)

    if shard % 128 != 0:
        return attend_rows_narrow(normed_all, back, extra)
    return pl.pallas_call(
        kernel,
        grid=(groups,),
        in_specs=[
            pl.BlockSpec((length, D), lambda i: (0, 0)),
            pl.BlockSpec((length, width), lambda i: (0, 0)),
        ]
        + [pl.BlockSpec((shard, more), lambda i: (i, 0))] * len(extra),
        out_specs=pl.BlockSpec((1, shard + EXTRA, width + more), lambda i: (i, 0, 0)),
        out_shape=jax.ShapeDtypeStruct((groups, shard + EXTRA, width + more), BF),
        scratch_shapes=[pltpu.VMEM((EXTRA, width), BF)],
        cost_estimate=about(5),
        compiler_params=pltpu.CompilerParams(vmem_limit_bytes=50 << 20),
        name="attend_rows",
    )(normed_all, in_hbm(back), *extra)


def attend_rows_narrow(normed_all, back, extra):
    groups = lax.axis_size("dp")
    grads = dot(normed_all, back, 0, 0)
    total = jnp.sum(back.astype(F32), axis=0)
    addends = []
    for _ in range(3):
        addends.append(total.astype(BF))
        total = total - addends[-1].astype(F32)
    below = jnp.concatenate([jnp.stack(addends), jnp.zeros((EXTRA - 3, back.shape[1]), BF)], axis=0)
    if extra:
        grads = jnp.concatenate([grads, sum(value.astype(F32) for value in extra)], axis=1)
        below = jnp.concatenate([below, jnp.zeros((EXTRA, extra[0].shape[1]), BF)], axis=1)
    grads = grads.astype(BF).reshape(groups, D // groups, -1)
    below = jnp.broadcast_to(below[None], (groups,) + below.shape)
    return jnp.concatenate([grads, below], axis=1)


def attend_sums(piece, work, gains, width):
    groups, rows, columns = piece.shape
    shard = rows - EXTRA

    def kernel(piece_ref, work_ref, gain_ref, grad_ref, *outs):
        total = piece_ref[0].astype(F32)
        for k in range(1, groups):
            total = total + piece_ref[k].astype(F32)
        grad = total[:shard, :width]
        below = jnp.sum(total[shard:, :width], axis=0, keepdims=True)
        gain, bias = gain_ref[:, 0:1], gain_ref[:, 1:2]
        work = work_ref[...].astype(F32)
        grad_ref[...] = gain * grad + bias * below
        for k, value in enumerate((grad * work, below * work)):
            outs[0][:, k : k + 1] = jnp.sum(value, axis=1, keepdims=True)
        if columns > width:
            outs[1][...] = total[:shard, width:]

    outs = [((shard, width), F32), ((shard, 2), F32)]
    if columns > width:
        outs.append(((shard, columns - width), F32))
    return pl.pallas_call(
        kernel,
        in_specs=[vmem()] * 3,
        out_specs=[vmem()] * len(outs),
        out_shape=[jax.ShapeDtypeStruct(shape, kind) for shape, kind in outs],
        cost_estimate=about(2),
        compiler_params=pltpu.CompilerParams(vmem_limit_bytes=50 << 20),
        name="attend_sums",
    )(piece, work, gains)


def input_back(part, grads, work_in):
    width = grads[0].shape[1]

    def kernel(*refs):
        work_ref, outs = refs[len(grads)], refs[len(grads) + 1 :]
        term = dot(refs[0][...], work_ref[:, :width], 1, 1)
        for k in range(1, len(grads)):
            term = term + dot(refs[k][...], work_ref[:, k * width : (k + 1) * width], 1, 1)
        part.store(outs, term.astype(BF))

    return call(
        kernel,
        part,
        "input_back",
        [*grads, work_in],
        [part.whole(width)] * len(grads) + [fixed((D, len(grads) * width))],
        [((part.height, D), BF)] * len(part.blocks),
        part.pieces(D),
        pieces=True,
    )


def segments_at(rows, table_ref, count):
    slots = rows ^ table_ref[count]
    end = jnp.int32(0)
    segment = jnp.zeros(rows.shape, jnp.int32)
    for i in range(count):
        end = end + table_ref[i]
        segment = segment + (slots >= end).astype(jnp.int32)
    return segment


LANES = 128
PAIR = LANES // HD


def attention_forward(part, projected, table):
    length, width = projected.shape[0], projected.shape[1] // 3
    pairs = width // LANES
    block = part.height
    count = table.shape[0] - 2
    blocks = len(part.blocks)

    def kernel(table_ref, *refs):
        outs, log_ref, low = refs[3 * pairs : -2], refs[-2], refs[-1]
        start = pl.program_id(0) * block
        rows = start + lax.broadcasted_iota(jnp.int32, (block, 1), 0)
        columns = lax.broadcasted_iota(jnp.int32, (1, length), 1)
        allowed = segments_at(rows, table_ref, count) == segments_at(columns, table_ref, count)
        lane = lax.broadcasted_iota(jnp.int32, (1, LANES), 1) // HD
        def scores_of(p, h):
            query = refs[3 * p][...] * BF(HD**-0.5)
            one = jnp.where(lane == h, query, jnp.zeros_like(query))
            return jnp.where(allowed, dot(one, refs[3 * p + 1][...], 1, 1), MASKED)

        heads = [(p, h) for p in range(pairs) for h in range(PAIR)]
        following = scores_of(*heads[0])
        for k, (p, h) in enumerate(heads):
            scores = following
            if h == 0:
                out, logs = jnp.zeros((block, LANES), F32), []
            highest = jnp.max(scores, axis=1, keepdims=True)
            if k + 1 < len(heads):
                following = scores_of(*heads[k + 1])
            weights = jnp.exp(scores - highest).astype(BF)
            values = refs[3 * p + 2][...]
            mixed = dot(weights, jnp.where(lane == h, values, jnp.ones_like(values)), 1, 0)
            total = pltpu.roll(mixed, HD, axis=1)
            out = jnp.where(lane == h, mixed / total, out)
            logs.append(highest + jnp.log(total[:, h * HD : h * HD + 1]))
            if h == PAIR - 1:
                low[:, p * LANES : (p + 1) * LANES] = out.astype(BF)
                log_ref[8 * p : 8 * p + 8, :] = as_rows(logs, 8)
        part.store(outs, low[...])

    specs = []
    for p in range(pairs):
        specs.append(pl.BlockSpec((block, LANES), lambda i, t, p=p: (i, 3 * p)))
        specs.append(fixed((length, LANES), 0, 3 * p + 1))
        specs.append(fixed((length, LANES), 0, 3 * p + 2))
    *outs, logs = pl.pallas_call(
        kernel,
        grid_spec=pltpu.PrefetchScalarGridSpec(
            num_scalar_prefetch=1,
            grid=(blocks,),
            in_specs=specs,
            out_specs=part.pieces(width) + [pl.BlockSpec((8 * pairs, block), lambda i, t: (0, i))],
            scratch_shapes=[pltpu.VMEM((block, width), BF)],
        ),
        out_shape=[jax.ShapeDtypeStruct((block, width), BF)] * blocks
        + [jax.ShapeDtypeStruct((8 * pairs, length), F32)],
        cost_estimate=about(16 * pairs, 4.0),
        compiler_params=pltpu.CompilerParams(vmem_limit_bytes=48 << 20),
        name="attention_forward",
    )(table, *[in_hbm(projected)] * (3 * pairs))
    return outs, logs


def backward_kernel(
    table_ref, q_ref, k_ref, v_ref, log_ref, *refs, block, count
):
    out, sums, dots, grads = refs[-4:]
    blocks = (len(refs) - 4) // 2
    length = q_ref.shape[0]
    step = pl.program_id(0)
    lane = lax.broadcasted_iota(jnp.int32, (1, LANES), 1) // HD

    @pl.when(step == 0)
    def _():
        sums[...] = jnp.zeros_like(sums)
        for r in range(blocks):
            low, attended = refs[r][...], refs[blocks + r][...]
            height = low.shape[0]
            grads[r * height : (r + 1) * height, :] = low
            products = low.astype(F32) * attended.astype(F32)
            dots[:, r * height : (r + 1) * height] = as_rows(
                [
                    jnp.sum(jnp.where(lane == h, products, 0.0), axis=1, keepdims=True)
                    for h in range(PAIR)
                ],
                8,
            )

    grad = grads[...]
    start = pl.multiple_of(step * block, block)
    rows = start + lax.broadcasted_iota(jnp.int32, (block, 1), 0)
    columns = lax.broadcasted_iota(jnp.int32, (1, length), 1)
    allowed = segments_at(rows, table_ref, count) == segments_at(columns, table_ref, count)
    query = q_ref[...] * BF(HD**-0.5)
    keys = k_ref[...]
    values = v_ref[...]
    none = jnp.zeros_like(keys)
    key_back = jnp.zeros((block, LANES), F32)
    value_back = jnp.zeros((block, LANES), F32)
    for h in range(PAIR):
        key = jnp.where(lane == h, keys, none)
        value = jnp.where(lane == h, values, none)
        scores = jnp.where(allowed, dot(key, query, 1, 1), MASKED)
        probs = jnp.exp(scores - log_ref[h : h + 1, :])
        probs_back = dot(value, grad, 1, 1)
        score_back = (probs * (probs_back - dots[h : h + 1, :])).astype(BF)
        value_back = jnp.where(lane == h, dot(probs.astype(BF), grad, 1, 0), value_back)
        key_back = jnp.where(lane == h, dot(score_back, query, 1, 0), key_back)
        turned = jnp.transpose(keys)[h * HD : (h + 1) * HD]
        sums[h * HD : (h + 1) * HD, :] += dot(turned, score_back, 1, 0)
    out[pl.ds(start, block), LANES : 2 * LANES] = key_back.astype(BF)
    out[pl.ds(start, block), 2 * LANES :] = value_back.astype(BF)

    @pl.when(step == pl.num_programs(0) - 1)
    def _():
        out[:, :LANES] = (jnp.transpose(sums[...]) * HD**-0.5).astype(BF)


def attention_backward(pair, projected, table, grads, attended, logs):
    length = projected.shape[0]
    block = min(512, length)

    def column(c):
        return pl.BlockSpec((length, LANES), lambda i, t: (0, c))

    return pl.pallas_call(
        partial(backward_kernel, block=block, count=table.shape[0] - 2),
        grid_spec=pltpu.PrefetchScalarGridSpec(
            num_scalar_prefetch=1,
            grid=(length // block,),
            in_specs=[
                column(3 * pair),
                pl.BlockSpec((block, LANES), lambda i, t: (i, 3 * pair + 1)),
                pl.BlockSpec((block, LANES), lambda i, t: (i, 3 * pair + 2)),
                fixed((8, length), pair, 0),
            ]
            + [fixed((value.shape[0], LANES), 0, pair) for value in (*grads, *attended)],
            out_specs=fixed((length, 3 * LANES)),
            scratch_shapes=[
                pltpu.VMEM((LANES, length), F32),
                pltpu.VMEM((8, length), F32),
                pltpu.VMEM((length, LANES), BF),
            ],
        ),
        out_shape=jax.ShapeDtypeStruct((length, 3 * LANES), BF),
        cost_estimate=about(30, 4.0),
        compiler_params=pltpu.CompilerParams(vmem_limit_bytes=56 << 20),
        name="attention_backward",
    )(table, projected, projected, projected, logs, *grads, *attended)


def adamw_kernel(scale_ref, *refs, turned, parts):
    clip, fix_one, fix_two = scale_ref[0], scale_ref[1], scale_ref[2]
    step = pl.program_id(0)
    grads, ins, outs = refs[: 6 + parts], refs[6 + parts : 27 + parts], refs[27 + parts :]

    def update(k, grad):
        param, moment, square = (ref[...] for ref in ins[3 * k : 3 * k + 3])
        grad_ref, moment_ref, square_ref, change_ref = outs[4 * k : 4 * k + 4]
        clipped = grad * clip
        moment_new = BETA_ONE * moment + (1.0 - BETA_ONE) * clipped
        square_new = BETA_TWO * square + (1.0 - BETA_TWO) * clipped * clipped
        grad_ref[...] = grad
        moment_ref[...] = moment_new
        square_ref[...] = square_new
        change_ref[...] = -RATE * (
            moment_new / fix_one / (jnp.sqrt(square_new / fix_two) + ADAM_EPS) + DECAY * param
        )

    update(
        0,
        jnp.stack(
            [
                jnp.concatenate([ref[:, c * LANES : (c + 1) * LANES] for ref in grads[:parts]], axis=1)
                for c in range(3)
            ]
        ),
    )
    update(2, grads[parts + 1][...].astype(F32))
    update(3, jnp.transpose(grads[parts + 2][...].astype(F32)))

    @pl.when(step < turned)
    def _():
        update(1, jnp.transpose(grads[parts][...]))

    @pl.when(step == 0)
    def _():
        for k in range(3):
            update(4 + k, grads[parts + 3 + k][...])


def in_hbm(value):
    return pltpu.with_memory_space_constraint(value, pltpu.HBM)


def adamw(scales, attend_parts, others, params, firsts, squares):
    shard = params[0].shape[1]
    block = 2 * LANES
    mix_block = min(block, params[1].shape[0])
    steps = params[3].shape[0] // block
    turned = params[1].shape[0] // mix_block
    rows = shard // steps

    def last(i):
        return jnp.minimum(i, turned - 1)

    state = [
        pl.BlockSpec((3, rows, params[0].shape[2]), lambda i: (0, i, 0)),
        pl.BlockSpec((mix_block, shard), lambda i: (last(i), 0)),
        pl.BlockSpec((rows, params[2].shape[1]), lambda i: (i, 0)),
        pl.BlockSpec((block, shard), lambda i: (i, 0)),
    ] + [pl.BlockSpec(value.shape, lambda i: (0, 0)) for value in params[4:]]
    grad_specs = (
        [pl.BlockSpec((rows, 3 * LANES), lambda i: (i, 0)) for _ in attend_parts]
        + [
            pl.BlockSpec((shard, mix_block), lambda i: (0, last(i))),
            state[2],
            pl.BlockSpec((shard, block), lambda i: (0, i)),
        ]
        + state[4:]
    )
    ins = [in_hbm(value) for group in zip(params, firsts, squares) for value in group]
    return pl.pallas_call(
        partial(adamw_kernel, turned=turned, parts=len(attend_parts)),
        grid=(steps,),
        in_specs=[smem()] + grad_specs + [spec for spec in state for _ in range(3)],
        out_specs=[spec for spec in state for _ in range(4)],
        out_shape=[jax.ShapeDtypeStruct(value.shape, F32) for value in params for _ in range(4)],
        cost_estimate=about(6),
        compiler_params=pltpu.CompilerParams(vmem_limit_bytes=50 << 20),
        name="adamw",
    )(scales, *attend_parts, *others, *ins)


def local(
    tokens,
    cotangent,
    lengths,
    attend,
    mixing,
    expand,
    contract,
    outer_norms,
    head_norms,
    unit_norms,
    attend_moment,
    mixing_moment,
    expand_moment,
    contract_moment,
    outer_moment,
    head_moment,
    unit_moment,
    attend_square,
    mixing_square,
    expand_square,
    contract_square,
    outer_square,
    head_square,
    unit_square,
):
    height = tokens.shape[0]
    shard_count = lax.axis_size("mp")
    device_count = lax.axis_size("dp") * shard_count
    length_all = height * shard_count
    place = lax.axis_index("mp")
    sequences = lengths.shape[1]
    head_width = attend.shape[2]
    unit_width = expand.shape[1]
    shard = attend.shape[1]
    pairs = head_width // LANES
    step = height
    everything = Rows(list(range(shard_count)), height, step)
    near = Rows([0, 1], height, step)
    far = Rows(list(range(2, shard_count)), height, step)
    table = jnp.concatenate([lengths[0], jnp.stack([place * height, place]).astype(jnp.int32)])

    by_pair = attend.astype(BF).reshape(3, shard, pairs, LANES).transpose(1, 2, 0, 3)
    by_pair = by_pair.reshape(shard, 3 * head_width)
    work_even = gather_groups(jnp.concatenate([by_pair, mixing.astype(BF).T], axis=1))

    sizes = [x.size for x in (outer_norms, head_norms, unit_norms)]
    starts = [0, sizes[0], sizes[0] + sizes[1]]
    packed = jnp.concatenate([outer_norms.reshape(-1), head_norms.reshape(-1), unit_norms.reshape(-1)])
    tables = exchange_all(jnp.broadcast_to(packed[None], (device_count, packed.shape[0])))

    token_near, token_even = gather_near(tokens)
    wide_shard = jnp.concatenate([expand.astype(BF), contract.astype(BF).T], axis=1)
    work_odd = cross_groups(work_even, [*token_even, tables, wide_shard])
    token_far = gather_far(after(token_even, work_odd))
    work_in, work_mix = place_groups(work_even, work_odd, [3 * head_width, head_width])
    wide_shard = after([wide_shard], [*work_even[1:], tables])[0]
    weights = lax.all_gather(wide_shard, "dp", axis=0, tiled=True)

    def unpack(k, rows):
        part = tables[:, starts[k] : starts[k] + sizes[k]].reshape(device_count, rows, -1)
        return part.transpose(1, 0, 2).reshape(rows, -1)

    outer = unpack(0, 4)
    head_gains = unpack(1, 2)
    unit_local = lax.dynamic_slice_in_dim(unpack(2, 2), place * unit_width, unit_width, 1)
    normed_all, projected = project(everything, token_near + token_far, work_in, outer)
    mix_near, mix_even = gather_near(work_mix)
    attended, logs = attention_forward(everything, projected, table)
    back_near, back_even = gather_near(after([cotangent], [normed_all])[0])
    attended, logs, mix_near, mix_even, back_even = lax.optimization_barrier(
        (attended, logs, mix_near, mix_even, back_even)
    )
    mixes = mix_near + gather_far(mix_even)
    head_blocks = [attended[0]] + [swap(attended[r], r) for r in range(1, shard_count)]
    middle, mid_own, mixed_in = mix_rows(
        table, sequences, head_blocks, mixes, head_gains, tokens, outer
    )
    mid_near, mid_even = gather_near(mid_own)
    cotangent_blocks = back_near + gather_far(back_even)

    back_all, unit_in = feed_back(everything, cotangent_blocks, table, sequences, weights)
    kept = widen(near, mid_near, weights, unit_in, unit_local)
    mid_far = gather_far(after(mid_even, kept))
    mid_all, activated, slopes, sums = widen(far, mid_far, weights, unit_in, unit_local, kept)
    unit_totals = token_totals(sums)
    low_far, wide_far, sums_far, *far_terms = narrow_back(
        far, activated, slopes, unit_in, unit_totals, unit_local, weights
    )
    far_sums = [value.astype(BF) for value in sum_chip(far_terms)]
    arrived = sum_far(far_sums)
    late_slopes = after([slopes], far_sums)[0]
    unit_low, widened_low, sums_near, *near_terms = narrow_back(
        near, activated, late_slopes, unit_in, unit_totals, unit_local, weights, (low_far, wide_far)
    )
    contract_back = weight_grad(back_all, unit_low)
    arrived = after(arrived, [*near_terms, contract_back])
    mid_terms = [near_terms[0], swap(near_terms[1], 1), *arrived]
    middle_back, middle_low, outer_sums, head_sums, *head_grads = mix_rows_back(
        table, sequences, mid_terms, middle, cotangent, outer, head_blocks, mixes, head_gains
    )

    grad_even = [head_grads[0]] + [swap(head_grads[r], r) for r in range(1, shard_count)]
    feed_terms = feed_rows(everything, after([unit_low], [middle_low])[0], weights)
    expand_back = weight_grad(mid_all, after([widened_low], [middle_low])[0])
    mix_terms = mix_grads(middle_low, mixed_in, shard_count)
    grad_blocks = [grad_even[0]] + after(grad_even[1:], [*feed_terms, *mix_terms, expand_back])

    def column_sums(value):
        return jnp.sum(value.reshape(2, 8, -1), axis=1)

    def for_owners(value):
        return value.reshape(value.shape[0], device_count, -1).transpose(1, 0, 2).reshape(device_count, -1)

    unit_sums = lax.dynamic_update_slice_in_dim(
        jnp.zeros((2, FF), F32), column_sums(sums_near + sums_far), place * unit_width, 1
    )
    terms = jnp.concatenate(
        [
            for_owners(column_sums(outer_sums)),
            for_owners(column_sums(head_sums)),
            for_owners(unit_sums),
        ],
        axis=1,
    )
    feed_sums = [value.astype(BF) for value in sum_chip(feed_terms[2:])]
    mix_sums = [value.astype(BF) for value in sum_chip(mix_terms[2:])]
    grad_blocks = after(grad_blocks, [*feed_sums, *mix_sums])
    term_sums = exchange_all(after([terms], grad_blocks)[0])
    *mix_sums, last = after([*mix_sums, feed_sums[-1]], grad_blocks)
    mix_arrived = sum_far(mix_sums)
    feed_arrived = sum_far([*feed_sums[:-1], last])
    backs = [attention_backward(0, projected, table, grad_blocks, attended, logs)]
    backs, feed_arrived, mix_arrived, term_sums = lax.optimization_barrier(
        (backs, feed_arrived, mix_arrived, term_sums)
    )
    mix_terms = [mix_terms[0], swap(mix_terms[1], 1), *mix_arrived]
    pieces = [exchange_groups(attend_rows(normed_all, backs[0], mix_terms))]
    for pair in range(1, pairs):
        backs.append(attention_backward(pair, projected, table, grad_blocks, attended, logs))
        value = after([attend_rows(normed_all, backs[-1])], pieces)[0]
        pieces.append(exchange_groups(value))
        late = [in_hbm(back) for back in after(backs, [value])]

    def scatter(value):
        return lax.psum_scatter(value, "dp", scatter_dimension=0, tiled=True)

    contract_grad = scatter(contract_back)
    expand_grad = scatter(expand_back)
    if pairs == 1:
        late = backs
    far_terms = input_back(far, late, work_in)
    far_sums = [value.astype(BF) for value in sum_chip(far_terms)]
    near_terms = input_back(near, after(late, far_sums), work_in)
    arrived = sum_far(far_sums)
    outer, expand_late, contract_late, term_sums = after(
        [outer, expand_grad, contract_grad, term_sums], near_terms
    )

    local_squares = jnp.float32(0.0)
    for gradient in [expand_late, contract_late]:
        local_squares = local_squares + jnp.sum(jnp.square(gradient.astype(F32)))
    local_squares, near_terms, pieces = lax.optimization_barrier((local_squares, near_terms, pieces))
    norm_sums = jnp.sum(term_sums, axis=0)
    outer_rows = lax.dynamic_slice_in_dim(outer, lax.axis_index("dp") * shard, shard, 1).T
    attend_parts, outer_terms = [], 0.0
    for pair, piece in enumerate(pieces):
        grad, sums, *beside = attend_sums(
            piece, by_pair[:, 3 * LANES * pair : 3 * LANES * (pair + 1)], outer_rows, 3 * LANES
        )
        attend_parts.append(grad)
        outer_terms = outer_terms + sums
        if beside:
            mixing_grad = beside[0]
    outer_terms = outer_terms.T
    for bit in mp_bits():
        outer_terms = outer_terms + swap(outer_terms, bit)
    own_norms = outer_norms.shape[1]
    first_grad = lax.dynamic_slice_in_dim(outer_terms, place * own_norms, own_norms, 1)
    half = sizes[0] // 2
    norm_grads = [
        jnp.concatenate([first_grad, norm_sums[:half].reshape(2, own_norms)], axis=0),
        norm_sums[half : half + sizes[1]].reshape(head_norms.shape),
        norm_sums[half + sizes[1] :].reshape(unit_norms.shape),
    ]

    for gradient in [*norm_grads, mixing_grad, *attend_parts]:
        local_squares = local_squares + jnp.sum(gradient * gradient)
    all_squares = exchange_all(jnp.broadcast_to(local_squares, (device_count, 128)))
    result = middle + sum_near(feed_terms[:2], after(feed_arrived, [local_squares]))
    result = result.astype(BF)
    normed_back = sum_near(near_terms, arrived)
    inputs = tokens.astype(F32)
    first_normed, first_factor = norm_rows(inputs)
    input_grad = middle_back + norm_back(normed_back, first_normed, first_factor, outer[0])[0]
    all_squares, input_grad, result = lax.optimization_barrier((all_squares, input_grad, result))
    norm = jnp.sqrt(jnp.sum(all_squares[:, 0]))
    clip = jnp.minimum(1.0, MAX_NORM / (norm + 1e-06))
    count_steps = jnp.float32(ADAM_STEP)
    fix_one = 1.0 - jnp.power(jnp.float32(BETA_ONE), count_steps)
    fix_two = 1.0 - jnp.power(jnp.float32(BETA_TWO), count_steps)
    results = adamw(
        jnp.stack([clip, fix_one, fix_two]),
        attend_parts,
        [mixing_grad, expand_grad, contract_grad, *norm_grads],
        (attend, mixing, expand, contract, outer_norms, head_norms, unit_norms),
        (
            attend_moment,
            mixing_moment,
            expand_moment,
            contract_moment,
            outer_moment,
            head_moment,
            unit_moment,
        ),
        (
            attend_square,
            mixing_square,
            expand_square,
            contract_square,
            outer_square,
            head_square,
            unit_square,
        ),
    )
    return (result, input_grad, norm, *results)


def solution(mesh):
    rows = P(ALL, None)
    norms = P(None, ALL)
    weights = (P(None, "dp", "mp"), P("mp", "dp"), P("dp", "mp"), P("mp", "dp"))
    states = weights + (norms,) * 3
    outs = (rows, rows, P())
    for spec in states:
        outs = outs + (spec,) * 4
    return jax.shard_map(
        local,
        mesh=mesh,
        in_specs=(rows, rows, P("dp", None)) + states * 3,
        out_specs=outs,
        check_vma=False,
    )
```

```python
from functools import partial

import jax
import jax.numpy as jnp
from jax import lax
from jax.experimental import pallas as pl
from jax.experimental.pallas import tpu as pltpu
from jax.sharding import PartitionSpec as P

D = 1024
HD = 64
FF = 4096
ADAM_STEP = 10

NORM_EPS = 1e-05
MASKED = -1e30
RATE = 0.02
BETA_ONE = 0.9
BETA_TWO = 0.95
ADAM_EPS = 1e-08
DECAY = 0.1
MAX_NORM = 1.0

BF = jnp.bfloat16
F32 = jnp.float32
ALL = ("dp", "mp")


def swap(value, bit):
    count = lax.axis_size("mp")
    return lax.ppermute(value, "mp", [(i, i ^ bit) for i in range(count)])


def mp_bits():
    count = lax.axis_size("mp")
    return [1 << b for b in range(count.bit_length() - 1)]


def after(values, others):
    values, _ = lax.optimization_barrier((tuple(values), tuple(others)))
    return list(values)


def gather_near(own):
    even = {0: own}
    for bit in reversed(mp_bits()[1:]):
        for r in list(even):
            even[r | bit] = swap(even[r], bit)
    return [own, swap(own, 1)], [even[r] for r in range(2, 2 * len(even), 2)]


def gather_far(even):
    return [block for value in even for block in (value, swap(value, 1))]


def sum_chip(terms):
    return [
        terms[2 * i].astype(F32) + swap(terms[2 * i + 1], 1).astype(F32)
        for i in range(len(terms) // 2)
    ]


def sum_far(sums):
    even = {2 * i + 2: value for i, value in enumerate(sums)}
    arrived = []
    for bit in mp_bits()[1:]:
        for r in [r for r in even if r & bit]:
            received = swap(even.pop(r).astype(BF), bit)
            if r == bit:
                arrived.append(received)
            else:
                even[r ^ bit] = even[r ^ bit].astype(F32) + received.astype(F32)
    return arrived


def sum_near(terms, arrived):
    total = terms[0].astype(F32) + swap(terms[1], 1).astype(F32)
    for value in arrived:
        total = total + value.astype(F32)
    return total


def token_totals(values):
    count = lax.axis_size("mp")
    height = values.shape[1] // count
    for bit in mp_bits():
        received = swap(values, bit)
        parts = [received[:, (r ^ bit) * height : ((r ^ bit) + 1) * height] for r in range(count)]
        values = values + jnp.concatenate(parts, axis=1)
    return values


def exchange_all(value):
    return lax.all_to_all(value, ALL, 0, 0, tiled=True)


def dp_swap(value, bits):
    count = lax.axis_size("dp")
    return lax.ppermute(value, "dp", [(i, i ^ bits) for i in range(count)])


def place_kernel(table_ref, *refs):
    blocks, outs = refs[:8], refs[8:]
    rows = blocks[0].shape[0]
    for r, ref in enumerate(blocks):
        start = pl.multiple_of((table_ref[0] ^ r) * rows, rows)
        first = 0
        for out in outs:
            out[pl.ds(start, rows), :] = ref[:, first : first + out.shape[1]]
            first += out.shape[1]


def smem():
    return pl.BlockSpec(memory_space=pltpu.SMEM)


def vmem():
    return pl.BlockSpec(memory_space=pltpu.VMEM)


def gather_groups(shard):
    if lax.axis_size("dp") != 8:
        return [lax.all_gather(shard, "dp", axis=0, tiled=True)]
    return [shard] + [dp_swap(shard, bits) for bits in (2, 4, 6)]


def cross_groups(even, others):
    if len(even) == 1:
        return []
    first = dp_swap(even[0], 1)
    odd = [first, dp_swap(first, 2)]
    return odd + [dp_swap(value, 1) for value in after(even[2:], odd + even[1:2] + others)]


def place_groups(even, odd, widths):
    if len(even) == 1:
        return list(jnp.split(even[0], [sum(widths[: k + 1]) for k in range(len(widths) - 1)], axis=1))
    blocks = [block for both in zip(even, odd) for block in both]
    place = lax.axis_index("dp").astype(jnp.int32)[None]
    rows = even[0].shape[0]
    return pl.pallas_call(
        place_kernel,
        in_specs=[smem()] + [vmem()] * 8,
        out_specs=[vmem()] * len(widths),
        out_shape=[jax.ShapeDtypeStruct((8 * rows, width), even[0].dtype) for width in widths],
        cost_estimate=about(2),
        name="place_rows",
    )(place, *blocks)


def exchange_groups(value):
    return lax.all_to_all(value, "dp", 0, 0, tiled=True)


HINT = 4.0


def about(microseconds, hint=HINT):
    return pl.CostEstimate(
        flops=int(microseconds * hint * 1.15e9),
        transcendentals=0,
        bytes_accessed=int(microseconds * hint * 1e5),
    )


def dot(left, right, left_dim, right_dim):
    return lax.dot_general(
        left, right, (((left_dim,), (right_dim,)), ((), ())), preferred_element_type=F32
    )


def norm_rows(value):
    mean = jnp.mean(value, axis=-1, keepdims=True)
    centered = value - mean
    variance = jnp.mean(centered * centered, axis=-1, keepdims=True)
    factor = lax.rsqrt(variance + NORM_EPS)
    return centered * factor, factor


def norm_back(grad, normed, factor, gain):
    weighted = grad * gain
    result = factor * (
        weighted
        - jnp.mean(weighted, axis=-1, keepdims=True)
        - normed * jnp.mean(weighted * normed, axis=-1, keepdims=True)
    )
    return result, jnp.sum(grad * normed, axis=0), jnp.sum(grad, axis=0)


def as_rows(columns, count):
    rows = columns[0].shape[0]
    lane = lax.broadcasted_iota(jnp.int32, (rows, 128), 1)
    spread = jnp.zeros((rows, 128), F32)
    for i, column in enumerate(columns):
        spread = jnp.where(lane == i, column, spread)
    return jnp.transpose(spread)[:count]


def as_columns(values):
    count, rows = values.shape
    padded = jnp.concatenate([values, jnp.zeros((128 - count, rows), F32)], axis=0)
    turned = jnp.transpose(padded)
    return [turned[:, i : i + 1] for i in range(count)]


def fold(value):
    return jnp.sum(value.reshape(value.shape[0] // 8, 8, value.shape[1]), axis=0)


def moments(first, second, width):
    mean = first / width
    variance = second / width - mean * mean
    return mean, lax.rsqrt(variance + NORM_EPS)


class Rows:
    def __init__(self, blocks, height, step):
        self.blocks = blocks
        self.per = height // step
        self.step = step
        self.height = height
        self.grid = (len(blocks) * self.per,)

    def at(self, i):
        return i + self.blocks[0] * self.per

    def whole(self, width, column=0):
        return pl.BlockSpec((self.step, width), lambda i, *t: (self.at(i), column))

    def stats(self, count):
        return pl.BlockSpec((count, self.step), lambda i, *t: (0, self.at(i)))

    def pieces(self, width):
        per = self.per
        return [
            pl.BlockSpec(
                (self.step, width), lambda i, *t, first=k * per: (jnp.clip(i - first, 0, per - 1), 0)
            )
            for k in range(len(self.blocks))
        ]

    def load(self, refs, into):
        for k, ref in enumerate(refs):

            @pl.when(pl.program_id(0) // self.per == k)
            def _():
                into[...] = ref[...]

    def store(self, refs, value):
        for k, ref in enumerate(refs):

            @pl.when(pl.program_id(0) // self.per == k)
            def _():
                ref[...] = value


def fixed(shape, *index):
    index = index or (0,) * len(shape)
    return pl.BlockSpec(shape, lambda i, *t: index)


ANY = pl.BlockSpec(memory_space=pl.ANY)


def call(kernel, part, name, ins, in_specs, outs, out_specs, scratch=(), kept=None, table=None, cost=8, pieces=False):
    ins, in_specs = list(ins), list(in_specs)
    aliases = {}
    tables = [] if table is None else [table]
    if kept is not None:
        for k, value in enumerate(kept):
            aliases[len(tables) + len(ins)] = k
            ins.append(value)
            in_specs.append(ANY)
    dropped = 0 if kept is None else len(kept)
    used = len(tables) + len(ins) - dropped

    def body(*refs):
        kernel(*refs[:used], *refs[used + dropped :])

    hbm = len(outs) - len(part.blocks) if pieces else len(outs)
    return pl.pallas_call(
        body,
        grid_spec=pltpu.PrefetchScalarGridSpec(
            num_scalar_prefetch=len(tables),
            grid=part.grid,
            in_specs=in_specs,
            out_specs=list(out_specs),
            scratch_shapes=list(scratch),
        ),
        out_shape=[jax.ShapeDtypeStruct(*out) for out in outs[:hbm]]
        + [pltpu.HBM(*out) for out in outs[hbm:]],
        input_output_aliases=aliases,
        cost_estimate=about(cost * len(part.blocks) / 4),
        compiler_params=pltpu.CompilerParams(vmem_limit_bytes=50 << 20),
        name=name,
    )(*tables, *ins)


def project(part, blocks, work_in, outer):
    count, length = len(blocks), len(blocks) * part.height
    width = work_in.shape[1]

    def kernel(*refs):
        work_ref, gain_ref, normed_ref, out_ref, row = refs[count:]
        part.load(refs[:count], row)
        normed = norm_rows(row[...].astype(F32))[0]
        normed_ref[...] = normed.astype(BF)
        normed = (normed * gain_ref[0:1] + gain_ref[1:2]).astype(BF)
        out_ref[...] = dot(normed, work_ref[...], 1, 0).astype(BF)

    return call(
        kernel,
        part,
        "project",
        [*blocks, work_in, outer],
        [*part.pieces(D), fixed(work_in.shape), fixed(outer.shape)],
        [((length, D), BF), ((length, width), BF)],
        [part.whole(D), part.whole(width)],
        [pltpu.VMEM((part.step, D), BF)],
    )


def columns_of(table_ref, index, r, width):
    return pl.ds(pl.multiple_of((table_ref[index] ^ r) * width, width), width)


def head_norm(att_refs):
    parts = [ref[...].astype(F32) for ref in att_refs]
    mean = sum(jnp.sum(part, axis=1, keepdims=True) for part in parts) / D
    parts = [part - mean for part in parts]
    variance = sum(jnp.sum(part * part, axis=1, keepdims=True) for part in parts) / D
    factor = lax.rsqrt(variance + NORM_EPS)
    return [part * factor for part in parts], factor


def own_call(kernel, name, table, ins, in_specs, outs, out_specs, height, cost, scratch=()):
    return pl.pallas_call(
        kernel,
        grid_spec=pltpu.PrefetchScalarGridSpec(
            num_scalar_prefetch=1,
            grid=(height // OWN_STEP,),
            in_specs=in_specs,
            out_specs=out_specs,
            scratch_shapes=list(scratch),
        ),
        out_shape=[pltpu.HBM(*out) if out[1] == BF else jax.ShapeDtypeStruct(*out) for out in outs],
        cost_estimate=about(cost),
        compiler_params=pltpu.CompilerParams(vmem_limit_bytes=50 << 20),
        name=name,
    )(table, *ins)


OWN_STEP = 256


def own(width):
    return pl.BlockSpec((OWN_STEP, width), lambda i, t: (i, 0))


def mix_rows(table, sequences, blocks, mixes, gains, tokens, outer):
    count, (height, width) = len(blocks), blocks[0].shape

    def kernel(table_ref, *refs):
        att_refs, mix_refs = refs[:count], refs[count : 2 * count]
        gain_ref, token_ref, outer_ref, middle_ref, mid_ref, in_ref = refs[2 * count :]
        middle = token_ref[...].astype(F32)
        for r, normed in enumerate(head_norm(att_refs)[0]):
            columns = columns_of(table_ref, sequences + 1, r, width)
            low = (normed * gain_ref[0:1, columns] + gain_ref[1:2, columns]).astype(BF)
            in_ref[:, r * width : (r + 1) * width] = low
            middle = middle + dot(low, mix_refs[r][...], 1, 1)
        middle_ref[...] = middle
        mid_ref[...] = (norm_rows(middle)[0] * outer_ref[2:3] + outer_ref[3:4]).astype(BF)

    return own_call(
        kernel,
        "mix_rows",
        table,
        [*blocks, *mixes, gains, tokens, outer],
        [own(width)] * count + [fixed((D, width))] * count + [fixed((2, D)), own(D), fixed((4, D))],
        [((height, D), F32), ((height, D), BF), ((height, D), BF)],
        [own(D)] * 3,
        height,
        6,
    )


def mix_rows_back(table, sequences, terms, middle, cotangent, outer, blocks, mixes, gains):
    count, (height, width) = len(blocks), blocks[0].shape

    def kernel(table_ref, *refs):
        term_refs, refs = refs[: len(terms)], refs[len(terms) :]
        middle_ref, back_ref, outer_ref, gain_ref = refs[:4]
        att_refs, mix_refs = refs[4 : 4 + count], refs[4 + count : 4 + 2 * count]
        out_ref, low_ref, outer_sum, head_sum, *outs = refs[4 + 2 * count :]

        @pl.when(pl.program_id(0) == 0)
        def _():
            outer_sum[...] = jnp.zeros_like(outer_sum)
            head_sum[...] = jnp.zeros_like(head_sum)

        grad = sum(ref[...].astype(F32) for ref in term_refs)
        normed, factor = norm_rows(middle_ref[...])
        weighted = grad * outer_ref[2:3]
        first = jnp.mean(weighted, axis=1, keepdims=True)
        second = jnp.mean(weighted * normed, axis=1, keepdims=True)
        outer_sum[0:8] += fold(grad * normed)
        outer_sum[8:16] += fold(grad)
        rows = pl.program_id(0) * OWN_STEP + lax.broadcasted_iota(jnp.int32, (OWN_STEP, 1), 0)
        live = segments_at(rows, table_ref, sequences) < sequences
        back = jnp.where(live, back_ref[...].astype(F32), 0.0)
        back = back + factor * (weighted - first - normed * second)
        out_ref[...] = back
        low = back.astype(BF)
        low_ref[...] = low
        normed, factor = head_norm(att_refs)
        weighted = []
        first, second = 0.0, 0.0
        for r in range(count):
            columns = columns_of(table_ref, sequences + 1, r, width)
            grad = dot(low, mix_refs[r][...], 1, 0)
            head_sum[0:8, columns] += fold(grad * normed[r])
            head_sum[8:16, columns] += fold(grad)
            weighted.append(grad * gain_ref[0:1, columns])
            first = first + jnp.sum(weighted[r], axis=1, keepdims=True)
            second = second + jnp.sum(weighted[r] * normed[r], axis=1, keepdims=True)
        for r in range(count):
            value = factor * (weighted[r] - first / D - normed[r] * (second / D))
            outs[r][...] = value.astype(BF)

    return own_call(
        kernel,
        "mix_rows_back",
        table,
        [*terms, middle, cotangent, outer, gains, *blocks, *mixes],
        [own(D)] * (len(terms) + 2)
        + [fixed((4, D)), fixed((2, D))]
        + [own(width)] * count
        + [fixed((D, width))] * count,
        [((height, D), F32), ((height, D), BF), ((16, D), F32), ((16, D), F32)]
        + [((height, width), BF)] * count,
        [own(D), own(D), fixed((16, D)), fixed((16, D))] + [own(width)] * count,
        height,
        8,
    )


def mix_grads(low, mixed_in, count):
    height, width = low.shape[0], mixed_in.shape[1] // count
    block = 256

    def kernel(low_ref, in_ref, *outs):
        for r in range(count):
            outs[r][...] = dot(low_ref[...], in_ref[:, r * width : (r + 1) * width], 0, 0).astype(BF)

    return pl.pallas_call(
        kernel,
        grid=(D // block,),
        in_specs=[
            pl.BlockSpec((height, block), lambda i: (0, i)),
            pl.BlockSpec((height, D), lambda i: (0, 0)),
        ],
        out_specs=[pl.BlockSpec((block, width), lambda i: (i, 0))] * count,
        out_shape=[pltpu.HBM((D, width), BF)] * count,
        cost_estimate=about(4),
        compiler_params=pltpu.CompilerParams(vmem_limit_bytes=50 << 20),
        name="mix_grads",
    )(low, mixed_in)


def feed_back(part, blocks, table, sequences, weights):
    count, length = len(blocks), len(blocks) * part.height
    units = weights.shape[1] // 2

    def kernel(table_ref, *refs):
        work_ref, back_ref, out_ref, row = refs[count:]
        part.load(refs[:count], row)
        rows = pl.program_id(0) * part.step + lax.broadcasted_iota(jnp.int32, (part.step, 1), 0)
        live = segments_at(rows, table_ref, sequences) < sequences
        back = jnp.where(live, row[...].astype(F32), 0.0).astype(BF)
        back_ref[...] = back
        out_ref[...] = dot(back, work_ref[...], 1, 0).astype(BF)

    return call(
        kernel,
        part,
        "feed_back",
        [*blocks, weights],
        [*part.pieces(D), fixed((D, units), 0, 1)],
        [((length, D), BF), ((length, units), BF)],
        [part.whole(D), part.whole(units)],
        [pltpu.VMEM((part.step, D), BF)],
        table=table,
    )


def widen(part, blocks, weights, unit_in, gains, kept=None):
    count, (length, units) = len(blocks), unit_in.shape

    def kernel(*refs):
        work_ref, in_ref, gain_ref, mid_ref, act_ref, slope_ref, total_ref, row = refs[count:]
        part.load(refs[:count], row)
        mid_ref[...] = row[...]
        wide = dot(row[...], work_ref[...], 1, 0)
        share = 0.5 + 0.5 * lax.erf(wide * 0.7071067811865476)
        act = wide * share
        act_ref[...] = act
        slope_ref[...] = (share + wide * (0.3989422804014327 * jnp.exp(-0.5 * wide * wide))).astype(BF)
        weighted = in_ref[...].astype(F32) * gain_ref[0:1]
        values = (act, act * act, weighted, weighted * act)
        total_ref[...] = as_rows([jnp.sum(v, axis=1, keepdims=True) for v in values], 4)

    return call(
        kernel,
        part,
        "widen",
        [*blocks, weights, unit_in, gains],
        [*part.pieces(D), fixed((D, units), 0, 0), part.whole(units), fixed(gains.shape)],
        [((length, D), BF), ((length, units), F32), ((length, units), BF), ((4, length), F32)],
        [part.whole(D), part.whole(units), part.whole(units), part.stats(4)],
        [pltpu.VMEM((part.step, D), BF)],
        kept=kept,
    )


NARROW_ROWS = 64
NARROW_COLUMNS = 256


def narrow_back(part, act, slope, unit_in, totals, gains, weights, kept=None):
    length, units = act.shape

    def kernel(act_ref, slope_ref, in_ref, total_ref, gain_ref, work_ref, low_ref, wide_ref, sum_ref, *outs):
        first, second, third, fourth = as_columns(total_ref[...])
        mean, factor = moments(first, second, FF)
        inner = factor * (fourth - mean * third)

        @pl.when(pl.program_id(0) == 0)
        def _():
            sum_ref[...] = jnp.zeros_like(sum_ref)

        for start in range(0, part.step, NARROW_ROWS):
            rows = slice(start, start + NARROW_ROWS)
            for left in range(0, units, NARROW_COLUMNS):
                columns = slice(left, left + NARROW_COLUMNS)
                gain, bias = gain_ref[0:1, columns], gain_ref[1:2, columns]
                normed = (act_ref[rows, columns] - mean[rows]) * factor[rows]
                low_ref[rows, columns] = (normed * gain + bias).astype(BF)
                grad = in_ref[rows, columns].astype(F32)
                back = factor[rows] * (grad * gain - third[rows] / FF - normed * (inner[rows] / FF))
                wide_ref[rows, columns] = (back * slope_ref[rows, columns].astype(F32)).astype(BF)
                sum_ref[0:8, columns] += fold(grad * normed)
                sum_ref[8:16, columns] += fold(grad)
        part.store(outs, dot(wide_ref[...], work_ref[...], 1, 1).astype(BF))

    return call(
        kernel,
        part,
        "narrow_back",
        [act, slope, unit_in, totals, gains, weights],
        [part.whole(units)] * 3 + [part.stats(4), fixed(gains.shape), fixed((D, units), 0, 0)],
        [((length, units), BF)] * 2
        + [((16, units), F32)]
        + [((part.height, D), BF)] * len(part.blocks),
        [part.whole(units)] * 2 + [fixed((16, units))] + part.pieces(D),
        kept=kept,
        pieces=True,
    )


def weight_grad(left, right):
    length, block = left.shape[0], 256

    def kernel(left_ref, right_ref, out_ref):
        out_ref[...] = dot(left_ref[...], right_ref[...], 0, 0).astype(BF)

    return pl.pallas_call(
        kernel,
        grid=(left.shape[1] // block,),
        in_specs=[
            pl.BlockSpec((length, block), lambda i: (0, i)),
            pl.BlockSpec(right.shape, lambda i: (0, 0)),
        ],
        out_specs=pl.BlockSpec((block, right.shape[1]), lambda i: (i, 0)),
        out_shape=jax.ShapeDtypeStruct((left.shape[1], right.shape[1]), BF),
        cost_estimate=about(8),
        compiler_params=pltpu.CompilerParams(vmem_limit_bytes=50 << 20),
        name="weight_grad",
    )(left, right)


def feed_rows(part, low, weights):
    units = low.shape[1]

    def kernel(low_ref, work_ref, *outs):
        part.store(outs, dot(low_ref[...], work_ref[...], 1, 1).astype(BF))

    return call(
        kernel,
        part,
        "feed_rows",
        [low, weights],
        [part.whole(units), fixed((D, units), 0, 1)],
        [((part.height, D), BF)] * len(part.blocks),
        part.pieces(D),
        pieces=True,
    )


EXTRA = 16


def attend_rows(normed_all, back, extra=()):
    length, width = back.shape
    groups = lax.axis_size("dp")
    shard = D // groups
    more = extra[0].shape[1] if extra else 0

    def kernel(normed_ref, back_ref, *refs):
        out_ref, total_ref = refs[-2:]

        @pl.when(pl.program_id(0) == 0)
        def _():
            value = jnp.sum(fold(back_ref[...].astype(F32)), axis=0, keepdims=True)
            row = lax.broadcasted_iota(jnp.int32, (EXTRA, width), 0)
            total = jnp.zeros((EXTRA, width), F32)
            for k in range(3):
                piece = value.astype(BF).astype(F32)
                total = jnp.where(row == k, piece, total)
                value = value - piece
            total_ref[...] = total.astype(BF)

        start = pl.multiple_of(pl.program_id(0) * shard, shard)
        if shard % 128 == 0:
            normed = normed_ref[:, pl.ds(start, shard)]
        else:
            normed = normed_ref[...]
        out_ref[0, :shard, :width] = dot(normed, back_ref[...], 0, 0).astype(BF)
        out_ref[0, shard:, :width] = total_ref[...]
        if extra:
            value = sum(ref[...].astype(F32) for ref in refs[:-2])
            out_ref[0, :shard, width:] = value.astype(BF)
            out_ref[0, shard:, width:] = jnp.zeros((EXTRA, more), BF)

    if shard % 128 != 0:
        return attend_rows_narrow(normed_all, back, extra)
    return pl.pallas_call(
        kernel,
        grid=(groups,),
        in_specs=[
            pl.BlockSpec((length, D), lambda i: (0, 0)),
            pl.BlockSpec((length, width), lambda i: (0, 0)),
        ]
        + [pl.BlockSpec((shard, more), lambda i: (i, 0))] * len(extra),
        out_specs=pl.BlockSpec((1, shard + EXTRA, width + more), lambda i: (i, 0, 0)),
        out_shape=jax.ShapeDtypeStruct((groups, shard + EXTRA, width + more), BF),
        scratch_shapes=[pltpu.VMEM((EXTRA, width), BF)],
        cost_estimate=about(5),
        compiler_params=pltpu.CompilerParams(vmem_limit_bytes=50 << 20),
        name="attend_rows",
    )(normed_all, in_hbm(back), *extra)


def attend_rows_narrow(normed_all, back, extra):
    groups = lax.axis_size("dp")
    grads = dot(normed_all, back, 0, 0)
    total = jnp.sum(back.astype(F32), axis=0)
    addends = []
    for _ in range(3):
        addends.append(total.astype(BF))
        total = total - addends[-1].astype(F32)
    below = jnp.concatenate([jnp.stack(addends), jnp.zeros((EXTRA - 3, back.shape[1]), BF)], axis=0)
    if extra:
        grads = jnp.concatenate([grads, sum(value.astype(F32) for value in extra)], axis=1)
        below = jnp.concatenate([below, jnp.zeros((EXTRA, extra[0].shape[1]), BF)], axis=1)
    grads = grads.astype(BF).reshape(groups, D // groups, -1)
    below = jnp.broadcast_to(below[None], (groups,) + below.shape)
    return jnp.concatenate([grads, below], axis=1)


def lanes(value):
    return sum(value[:, i : i + LANES] for i in range(0, value.shape[1], LANES))


def attend_sums(piece, work, gains, width):
    groups, rows, columns = piece.shape
    shard = rows - EXTRA

    def kernel(piece_ref, work_ref, gain_ref, grad_ref, *outs):
        total = piece_ref[0].astype(F32)
        for k in range(1, groups):
            total = total + piece_ref[k].astype(F32)
        grad = total[:shard, :width]
        below = jnp.sum(total[shard:, :width], axis=0, keepdims=True)
        gain, bias = gain_ref[:, 0:1], gain_ref[:, 1:2]
        work = work_ref[...].astype(F32)
        result = gain * grad + bias * below
        grad_ref[...] = result
        squares = lanes(fold(result * result))
        for k, value in enumerate((grad * work, below * work)):
            outs[0][:, k : k + 1] = jnp.sum(value, axis=1, keepdims=True)
        if columns > width:
            value = total[:shard, width:]
            outs[2][...] = value
            squares = squares + lanes(fold(value * value))
        outs[1][...] = squares

    outs = [((shard, width), F32), ((shard, 2), F32), ((8, LANES), F32)]
    if columns > width:
        outs.append(((shard, columns - width), F32))
    return pl.pallas_call(
        kernel,
        in_specs=[vmem()] * 3,
        out_specs=[vmem()] * len(outs),
        out_shape=[jax.ShapeDtypeStruct(shape, kind) for shape, kind in outs],
        cost_estimate=about(2),
        compiler_params=pltpu.CompilerParams(vmem_limit_bytes=50 << 20),
        name="attend_sums",
    )(piece, work, gains)


def input_back(part, grads, work_in):
    width = grads[0].shape[1]

    def kernel(*refs):
        work_ref, outs = refs[len(grads)], refs[len(grads) + 1 :]
        term = dot(refs[0][...], work_ref[:, :width], 1, 1)
        for k in range(1, len(grads)):
            term = term + dot(refs[k][...], work_ref[:, k * width : (k + 1) * width], 1, 1)
        part.store(outs, term.astype(BF))

    return call(
        kernel,
        part,
        "input_back",
        [*grads, work_in],
        [part.whole(width)] * len(grads) + [fixed((D, len(grads) * width))],
        [((part.height, D), BF)] * len(part.blocks),
        part.pieces(D),
        pieces=True,
    )


def segments_at(rows, table_ref, count):
    slots = rows ^ table_ref[count]
    end = jnp.int32(0)
    segment = jnp.zeros(rows.shape, jnp.int32)
    for i in range(count):
        end = end + table_ref[i]
        segment = segment + (slots >= end).astype(jnp.int32)
    return segment


LANES = 128
PAIR = LANES // HD


def attention_forward(part, projected, table):
    length, width = projected.shape[0], projected.shape[1] // 3
    pairs = width // LANES
    block = part.height
    count = table.shape[0] - 2
    blocks = len(part.blocks)

    def kernel(table_ref, *refs):
        outs, log_ref, low = refs[3 * pairs : -2], refs[-2], refs[-1]
        start = pl.program_id(0) * block
        rows = start + lax.broadcasted_iota(jnp.int32, (block, 1), 0)
        columns = lax.broadcasted_iota(jnp.int32, (1, length), 1)
        allowed = segments_at(rows, table_ref, count) == segments_at(columns, table_ref, count)
        lane = lax.broadcasted_iota(jnp.int32, (1, LANES), 1) // HD
        def scores_of(p, h):
            query = refs[3 * p][...] * BF(HD**-0.5)
            one = jnp.where(lane == h, query, jnp.zeros_like(query))
            return jnp.where(allowed, dot(one, refs[3 * p + 1][...], 1, 1), MASKED)

        heads = [(p, h) for p in range(pairs) for h in range(PAIR)]
        following = scores_of(*heads[0])
        for k, (p, h) in enumerate(heads):
            scores = following
            if h == 0:
                out, logs = jnp.zeros((block, LANES), F32), []
            highest = jnp.max(scores, axis=1, keepdims=True)
            if k + 1 < len(heads):
                following = scores_of(*heads[k + 1])
            weights = jnp.exp(scores - highest).astype(BF)
            values = refs[3 * p + 2][...]
            mixed = dot(weights, jnp.where(lane == h, values, jnp.ones_like(values)), 1, 0)
            total = pltpu.roll(mixed, HD, axis=1)
            out = jnp.where(lane == h, mixed / total, out)
            logs.append(highest + jnp.log(total[:, h * HD : h * HD + 1]))
            if h == PAIR - 1:
                low[:, p * LANES : (p + 1) * LANES] = out.astype(BF)
                log_ref[8 * p : 8 * p + 8, :] = as_rows(logs, 8)
        part.store(outs, low[...])

    specs = []
    for p in range(pairs):
        specs.append(pl.BlockSpec((block, LANES), lambda i, t, p=p: (i, 3 * p)))
        specs.append(fixed((length, LANES), 0, 3 * p + 1))
        specs.append(fixed((length, LANES), 0, 3 * p + 2))
    *outs, logs = pl.pallas_call(
        kernel,
        grid_spec=pltpu.PrefetchScalarGridSpec(
            num_scalar_prefetch=1,
            grid=(blocks,),
            in_specs=specs,
            out_specs=part.pieces(width) + [pl.BlockSpec((8 * pairs, block), lambda i, t: (0, i))],
            scratch_shapes=[pltpu.VMEM((block, width), BF)],
        ),
        out_shape=[jax.ShapeDtypeStruct((block, width), BF)] * blocks
        + [jax.ShapeDtypeStruct((8 * pairs, length), F32)],
        cost_estimate=about(16 * pairs, 4.0),
        compiler_params=pltpu.CompilerParams(vmem_limit_bytes=48 << 20),
        name="attention_forward",
    )(table, *[in_hbm(projected)] * (3 * pairs))
    return outs, logs


def backward_kernel(
    table_ref, q_ref, k_ref, v_ref, log_ref, *refs, block, count
):
    out, sums, dots, grads = refs[-4:]
    blocks = (len(refs) - 4) // 2
    length = q_ref.shape[0]
    step = pl.program_id(0)
    lane = lax.broadcasted_iota(jnp.int32, (1, LANES), 1) // HD

    @pl.when(step == 0)
    def _():
        sums[...] = jnp.zeros_like(sums)
        for r in range(blocks):
            low, attended = refs[r][...], refs[blocks + r][...]
            height = low.shape[0]
            grads[r * height : (r + 1) * height, :] = low
            products = low.astype(F32) * attended.astype(F32)
            dots[:, r * height : (r + 1) * height] = as_rows(
                [
                    jnp.sum(jnp.where(lane == h, products, 0.0), axis=1, keepdims=True)
                    for h in range(PAIR)
                ],
                8,
            )

    grad = grads[...]
    start = pl.multiple_of(step * block, block)
    rows = start + lax.broadcasted_iota(jnp.int32, (block, 1), 0)
    columns = lax.broadcasted_iota(jnp.int32, (1, length), 1)
    allowed = segments_at(rows, table_ref, count) == segments_at(columns, table_ref, count)
    query = q_ref[...] * BF(HD**-0.5)
    keys = k_ref[...]
    values = v_ref[...]
    none = jnp.zeros_like(keys)
    key_back = jnp.zeros((block, LANES), F32)
    value_back = jnp.zeros((block, LANES), F32)
    for h in range(PAIR):
        key = jnp.where(lane == h, keys, none)
        value = jnp.where(lane == h, values, none)
        scores = jnp.where(allowed, dot(key, query, 1, 1), MASKED)
        probs = jnp.exp(scores - log_ref[h : h + 1, :])
        probs_back = dot(value, grad, 1, 1)
        score_back = (probs * (probs_back - dots[h : h + 1, :])).astype(BF)
        value_back = jnp.where(lane == h, dot(probs.astype(BF), grad, 1, 0), value_back)
        key_back = jnp.where(lane == h, dot(score_back, query, 1, 0), key_back)
        turned = jnp.transpose(keys)[h * HD : (h + 1) * HD]
        sums[h * HD : (h + 1) * HD, :] += dot(turned, score_back, 1, 0)
    out[pl.ds(start, block), LANES : 2 * LANES] = key_back.astype(BF)
    out[pl.ds(start, block), 2 * LANES :] = value_back.astype(BF)

    @pl.when(step == pl.num_programs(0) - 1)
    def _():
        out[:, :LANES] = (jnp.transpose(sums[...]) * HD**-0.5).astype(BF)


def attention_backward(pair, projected, table, grads, attended, logs):
    length = projected.shape[0]
    block = min(512, length)

    def column(c):
        return pl.BlockSpec((length, LANES), lambda i, t: (0, c))

    return pl.pallas_call(
        partial(backward_kernel, block=block, count=table.shape[0] - 2),
        grid_spec=pltpu.PrefetchScalarGridSpec(
            num_scalar_prefetch=1,
            grid=(length // block,),
            in_specs=[
                column(3 * pair),
                pl.BlockSpec((block, LANES), lambda i, t: (i, 3 * pair + 1)),
                pl.BlockSpec((block, LANES), lambda i, t: (i, 3 * pair + 2)),
                fixed((8, length), pair, 0),
            ]
            + [fixed((value.shape[0], LANES), 0, pair) for value in (*grads, *attended)],
            out_specs=fixed((length, 3 * LANES)),
            scratch_shapes=[
                pltpu.VMEM((LANES, length), F32),
                pltpu.VMEM((8, length), F32),
                pltpu.VMEM((length, LANES), BF),
            ],
        ),
        out_shape=jax.ShapeDtypeStruct((length, 3 * LANES), BF),
        cost_estimate=about(30, 4.0),
        compiler_params=pltpu.CompilerParams(vmem_limit_bytes=56 << 20),
        name="attention_backward",
    )(table, projected, projected, projected, logs, *grads, *attended)


def adamw_kernel(scale_ref, *refs, turned, parts):
    clip, fix_one, fix_two = scale_ref[0], scale_ref[1], scale_ref[2]
    step = pl.program_id(0)
    grads, ins, outs = refs[: 6 + parts], refs[6 + parts : 27 + parts], refs[27 + parts :]

    def update(k, grad):
        param, moment, square = (ref[...] for ref in ins[3 * k : 3 * k + 3])
        grad_ref, moment_ref, square_ref, change_ref = outs[4 * k : 4 * k + 4]
        clipped = grad * clip
        moment_new = BETA_ONE * moment + (1.0 - BETA_ONE) * clipped
        square_new = BETA_TWO * square + (1.0 - BETA_TWO) * clipped * clipped
        grad_ref[...] = grad
        moment_ref[...] = moment_new
        square_ref[...] = square_new
        change_ref[...] = -RATE * (
            moment_new / fix_one / (jnp.sqrt(square_new / fix_two) + ADAM_EPS) + DECAY * param
        )

    update(
        0,
        jnp.stack(
            [
                jnp.concatenate([ref[:, c * LANES : (c + 1) * LANES] for ref in grads[:parts]], axis=1)
                for c in range(3)
            ]
        ),
    )
    update(2, grads[parts + 1][...].astype(F32))
    update(3, jnp.transpose(grads[parts + 2][...].astype(F32)))

    @pl.when(step < turned)
    def _():
        update(1, jnp.transpose(grads[parts][...]))

    @pl.when(step == 0)
    def _():
        for k in range(3):
            update(4 + k, grads[parts + 3 + k][...])


def in_hbm(value):
    return pltpu.with_memory_space_constraint(value, pltpu.HBM)


def adamw(scales, attend_parts, others, params, firsts, squares):
    shard = params[0].shape[1]
    block = 2 * LANES
    mix_block = min(block, params[1].shape[0])
    steps = params[3].shape[0] // block
    turned = params[1].shape[0] // mix_block
    rows = shard // steps

    def last(i):
        return jnp.minimum(i, turned - 1)

    state = [
        pl.BlockSpec((3, rows, params[0].shape[2]), lambda i: (0, i, 0)),
        pl.BlockSpec((mix_block, shard), lambda i: (last(i), 0)),
        pl.BlockSpec((rows, params[2].shape[1]), lambda i: (i, 0)),
        pl.BlockSpec((block, shard), lambda i: (i, 0)),
    ] + [pl.BlockSpec(value.shape, lambda i: (0, 0)) for value in params[4:]]
    grad_specs = (
        [pl.BlockSpec((rows, 3 * LANES), lambda i: (i, 0)) for _ in attend_parts]
        + [
            pl.BlockSpec((shard, mix_block), lambda i: (0, last(i))),
            state[2],
            pl.BlockSpec((shard, block), lambda i: (0, i)),
        ]
        + state[4:]
    )
    ins = [in_hbm(value) for group in zip(params, firsts, squares) for value in group]
    return pl.pallas_call(
        partial(adamw_kernel, turned=turned, parts=len(attend_parts)),
        grid=(steps,),
        in_specs=[smem()] + grad_specs + [spec for spec in state for _ in range(3)],
        out_specs=[spec for spec in state for _ in range(4)],
        out_shape=[jax.ShapeDtypeStruct(value.shape, F32) for value in params for _ in range(4)],
        cost_estimate=about(6),
        compiler_params=pltpu.CompilerParams(vmem_limit_bytes=50 << 20),
        name="adamw",
    )(scales, *attend_parts, *others, *ins)


def local(
    tokens,
    cotangent,
    lengths,
    attend,
    mixing,
    expand,
    contract,
    outer_norms,
    head_norms,
    unit_norms,
    attend_moment,
    mixing_moment,
    expand_moment,
    contract_moment,
    outer_moment,
    head_moment,
    unit_moment,
    attend_square,
    mixing_square,
    expand_square,
    contract_square,
    outer_square,
    head_square,
    unit_square,
):
    height = tokens.shape[0]
    shard_count = lax.axis_size("mp")
    device_count = lax.axis_size("dp") * shard_count
    length_all = height * shard_count
    place = lax.axis_index("mp")
    sequences = lengths.shape[1]
    head_width = attend.shape[2]
    unit_width = expand.shape[1]
    shard = attend.shape[1]
    pairs = head_width // LANES
    step = height
    everything = Rows(list(range(shard_count)), height, step)
    near = Rows([0, 1], height, step)
    far = Rows(list(range(2, shard_count)), height, step)
    table = jnp.concatenate([lengths[0], jnp.stack([place * height, place]).astype(jnp.int32)])

    by_pair = attend.astype(BF).reshape(3, shard, pairs, LANES).transpose(1, 2, 0, 3)
    by_pair = by_pair.reshape(shard, 3 * head_width)
    work_even = gather_groups(jnp.concatenate([by_pair, mixing.astype(BF).T], axis=1))

    sizes = [x.size for x in (outer_norms, head_norms, unit_norms)]
    starts = [0, sizes[0], sizes[0] + sizes[1]]
    packed = jnp.concatenate([outer_norms.reshape(-1), head_norms.reshape(-1), unit_norms.reshape(-1)])
    tables = exchange_all(jnp.broadcast_to(packed[None], (device_count, packed.shape[0])))

    token_near, token_even = gather_near(tokens)
    wide_shard = jnp.concatenate([expand.astype(BF), contract.astype(BF).T], axis=1)
    work_odd = cross_groups(work_even, [*token_even, tables, wide_shard])
    token_far = gather_far(after(token_even, work_odd))
    work_in, work_mix = place_groups(work_even, work_odd, [3 * head_width, head_width])
    wide_shard = after([wide_shard], [*work_even[1:], tables])[0]
    weights = lax.all_gather(wide_shard, "dp", axis=0, tiled=True)

    def unpack(k, rows):
        part = tables[:, starts[k] : starts[k] + sizes[k]].reshape(device_count, rows, -1)
        return part.transpose(1, 0, 2).reshape(rows, -1)

    outer = unpack(0, 4)
    head_gains = unpack(1, 2)
    unit_local = lax.dynamic_slice_in_dim(unpack(2, 2), place * unit_width, unit_width, 1)
    normed_all, projected = project(everything, token_near + token_far, work_in, outer)
    mix_near, mix_even = gather_near(work_mix)
    attended, logs = attention_forward(everything, projected, table)
    back_near, back_even = gather_near(after([cotangent], [normed_all])[0])
    attended, logs, mix_near, mix_even, back_even = lax.optimization_barrier(
        (attended, logs, mix_near, mix_even, back_even)
    )
    mixes = mix_near + gather_far(mix_even)
    head_blocks = [attended[0]] + [swap(attended[r], r) for r in range(1, shard_count)]
    middle, mid_own, mixed_in = mix_rows(
        table, sequences, head_blocks, mixes, head_gains, tokens, outer
    )
    mid_near, mid_even = gather_near(mid_own)
    cotangent_blocks = back_near + gather_far(back_even)

    back_all, unit_in = feed_back(everything, cotangent_blocks, table, sequences, weights)
    kept = widen(near, mid_near, weights, unit_in, unit_local)
    mid_far = gather_far(after(mid_even, kept))
    mid_all, activated, slopes, sums = widen(far, mid_far, weights, unit_in, unit_local, kept)
    unit_totals = token_totals(sums)
    low_far, wide_far, sums_far, *far_terms = narrow_back(
        far, activated, slopes, unit_in, unit_totals, unit_local, weights
    )
    far_sums = [value.astype(BF) for value in sum_chip(far_terms)]
    arrived = sum_far(far_sums)
    late_slopes = after([slopes], far_sums)[0]
    unit_low, widened_low, sums_near, *near_terms = narrow_back(
        near, activated, late_slopes, unit_in, unit_totals, unit_local, weights, (low_far, wide_far)
    )
    contract_back = weight_grad(back_all, unit_low)
    arrived = after(arrived, [*near_terms, contract_back])
    mid_terms = [near_terms[0], swap(near_terms[1], 1), *arrived]
    middle_back, middle_low, outer_sums, head_sums, *head_grads = mix_rows_back(
        table, sequences, mid_terms, middle, cotangent, outer, head_blocks, mixes, head_gains
    )

    grad_even = [head_grads[0]] + [swap(head_grads[r], r) for r in range(1, shard_count)]
    feed_terms = feed_rows(everything, after([unit_low], [middle_low])[0], weights)
    expand_back = weight_grad(mid_all, after([widened_low], [middle_low])[0])
    mix_terms = mix_grads(middle_low, mixed_in, shard_count)
    grad_blocks = [grad_even[0]] + after(grad_even[1:], [*feed_terms, *mix_terms, expand_back])

    def column_sums(value):
        return jnp.sum(value.reshape(2, 8, -1), axis=1)

    def for_owners(value):
        return value.reshape(value.shape[0], device_count, -1).transpose(1, 0, 2).reshape(device_count, -1)

    unit_sums = lax.dynamic_update_slice_in_dim(
        jnp.zeros((2, FF), F32), column_sums(sums_near + sums_far), place * unit_width, 1
    )
    terms = jnp.concatenate(
        [
            for_owners(column_sums(outer_sums)),
            for_owners(column_sums(head_sums)),
            for_owners(unit_sums),
        ],
        axis=1,
    )
    feed_sums = [value.astype(BF) for value in sum_chip(feed_terms[2:])]
    mix_sums = [value.astype(BF) for value in sum_chip(mix_terms[2:])]
    grad_blocks = after(grad_blocks, [*feed_sums, *mix_sums])
    term_sums = exchange_all(after([terms], grad_blocks)[0])
    *mix_sums, last = after([*mix_sums, feed_sums[-1]], grad_blocks)
    mix_arrived = sum_far(mix_sums)
    feed_arrived = sum_far([*feed_sums[:-1], last])
    backs = [attention_backward(0, projected, table, grad_blocks, attended, logs)]
    backs, feed_arrived, mix_arrived, term_sums = lax.optimization_barrier(
        (backs, feed_arrived, mix_arrived, term_sums)
    )
    mix_terms = [mix_terms[0], swap(mix_terms[1], 1), *mix_arrived]
    pieces = [exchange_groups(attend_rows(normed_all, backs[0], mix_terms))]
    for pair in range(1, pairs):
        backs.append(attention_backward(pair, projected, table, grad_blocks, attended, logs))
        value = after([attend_rows(normed_all, backs[-1])], pieces)[0]
        pieces.append(exchange_groups(value))
        late = [in_hbm(back) for back in after(backs, [value])]

    def scatter(value):
        return lax.psum_scatter(value, "dp", scatter_dimension=0, tiled=True)

    contract_grad = scatter(contract_back)
    expand_grad = scatter(expand_back)
    if pairs == 1:
        late = backs
    far_terms = input_back(far, late, work_in)
    far_sums = [value.astype(BF) for value in sum_chip(far_terms)]
    near_terms = input_back(near, after(late, far_sums), work_in)
    arrived = sum_far(far_sums)
    outer, expand_late, contract_late, term_sums = after(
        [outer, expand_grad, contract_grad, term_sums], near_terms
    )

    local_squares = jnp.float32(0.0)
    for gradient in [expand_late, contract_late]:
        local_squares = local_squares + jnp.sum(jnp.square(gradient.astype(F32)))
    local_squares, near_terms, pieces = lax.optimization_barrier((local_squares, near_terms, pieces))
    norm_sums = jnp.sum(term_sums, axis=0)
    outer_rows = lax.dynamic_slice_in_dim(outer, lax.axis_index("dp") * shard, shard, 1).T
    attend_parts, outer_terms, all_parts = [], 0.0, 0.0
    for pair, piece in enumerate(pieces):
        grad, sums, part_squares, *beside = attend_sums(
            piece, by_pair[:, 3 * LANES * pair : 3 * LANES * (pair + 1)], outer_rows, 3 * LANES
        )
        attend_parts.append(grad)
        all_parts = all_parts + part_squares
        outer_terms = outer_terms + sums
        if beside:
            mixing_grad = beside[0]
    outer_terms = outer_terms.T
    for bit in mp_bits():
        outer_terms = outer_terms + swap(outer_terms, bit)
    own_norms = outer_norms.shape[1]
    first_grad = lax.dynamic_slice_in_dim(outer_terms, place * own_norms, own_norms, 1)
    half = sizes[0] // 2
    norm_grads = [
        jnp.concatenate([first_grad, norm_sums[:half].reshape(2, own_norms)], axis=0),
        norm_sums[half : half + sizes[1]].reshape(head_norms.shape),
        norm_sums[half + sizes[1] :].reshape(unit_norms.shape),
    ]

    local_squares = local_squares + jnp.sum(all_parts)
    for gradient in norm_grads:
        local_squares = local_squares + jnp.sum(gradient * gradient)
    all_squares = exchange_all(jnp.broadcast_to(local_squares, (device_count, 128)))
    result = middle + sum_near(feed_terms[:2], after(feed_arrived, [local_squares]))
    result = result.astype(BF)
    normed_back = sum_near(near_terms, arrived)
    inputs = tokens.astype(F32)
    first_normed, first_factor = norm_rows(inputs)
    input_grad = middle_back + norm_back(normed_back, first_normed, first_factor, outer[0])[0]
    all_squares, input_grad, result = lax.optimization_barrier((all_squares, input_grad, result))
    norm = jnp.sqrt(jnp.sum(all_squares[:, 0]))
    clip = jnp.minimum(1.0, MAX_NORM / (norm + 1e-06))
    count_steps = jnp.float32(ADAM_STEP)
    fix_one = 1.0 - jnp.power(jnp.float32(BETA_ONE), count_steps)
    fix_two = 1.0 - jnp.power(jnp.float32(BETA_TWO), count_steps)
    results = adamw(
        jnp.stack([clip, fix_one, fix_two]),
        attend_parts,
        [mixing_grad, expand_grad, contract_grad, *norm_grads],
        (attend, mixing, expand, contract, outer_norms, head_norms, unit_norms),
        (
            attend_moment,
            mixing_moment,
            expand_moment,
            contract_moment,
            outer_moment,
            head_moment,
            unit_moment,
        ),
        (
            attend_square,
            mixing_square,
            expand_square,
            contract_square,
            outer_square,
            head_square,
            unit_square,
        ),
    )
    return (result, input_grad, norm, *results)


def solution(mesh):
    rows = P(ALL, None)
    norms = P(None, ALL)
    weights = (P(None, "dp", "mp"), P("mp", "dp"), P("dp", "mp"), P("mp", "dp"))
    states = weights + (norms,) * 3
    outs = (rows, rows, P())
    for spec in states:
        outs = outs + (spec,) * 4
    return jax.shard_map(
        local,
        mesh=mesh,
        in_specs=(rows, rows, P("dp", None)) + states * 3,
        out_specs=outs,
        check_vma=False,
    )
```
